32 devices in a mesh: seq: 8 (over z, x), head: 4 (over y, core).
Axes of the slice: x: 2, y: 2, z: 4, core: 2. Of those that a mesh axis runs over, the one named last changes fastest.
Arguments:
- q_raw: bfloat16 [4096, 4096], P('seq', 'head'), may hold values from -120 to 120
- k_raw: bfloat16 [4096, 4096], P('seq', 'head'), may hold values from -6 to 6
- v_raw: bfloat16 [4096, 4096], P('seq', 'head'), may hold values from -6 to 6
- block_scales: float32 [3, 32, 32], P(None, 'seq', 'head'), may hold values from 0.25 to 4
- segment_ids: int32 [4096], P('seq'), may hold values from 0 to 24, as said below
- norm_gain: float32 [4096], P('head'), may hold values from 0.5 to 1.5
Outputs:
- attended: bfloat16 [4096, 4096], P('seq', 'head')
The draws below stay inside these ranges and needn't reach their ends.
Inputs may be any that keep to these rules, and one draw needn't show every extreme that they name: `segment_ids`: ids start at 0 and never fall, rising by at most one from a token to the next. Each aligned block of 512 tokens has exactly 4 segment starts, except the second and third blocks, which have none; in the second-to-last block all starts lie in the block's first half, in the last block all lie in its second half. No segment starts at the first token of a block except segment 0 at token 0.
All inputs are finite; a program needn't handle non-finite values.
Results may differ from the reference program's by a relative error of at most 0.013.
Values may be sent and summed in bfloat16 or wider, within the bound.
No kernel may reach another device: no remote copies, remote signals or barrier semaphores. Data moves between devices by JAX's collectives and lax.ppermute only.
A program may use at most 64 MiB of HBM per device.

```python
import math
import jax
import jax.numpy as jnp
from jax import lax

H = 32
HD = 128
TOK_DEV = 512
BLK = 128
CAP = 4
SEQ = 4096
N_SEQ = 8


def segment_draw(key):
    block_total = SEQ // TOK_DEV
    half_len = TOK_DEV // 2
    perm_key = jax.random.fold_in(key, 11)
    perm_keys = jax.random.split(perm_key, block_total)
    orders = jax.vmap(lambda subkey: jax.random.permutation(subkey, TOK_DEV - 1))(perm_keys).astype(jnp.int32)
    block_index = jnp.arange(block_total, dtype=jnp.int32)
    spots = jnp.arange(1, TOK_DEV, dtype=jnp.int32)
    last_block = (block_index == block_total - 1)[:, None]
    before_last = (block_index == block_total - 2)[:, None]
    early_spot = (spots < half_len)[None, :]
    pushed = last_block & early_spot | before_last & jnp.logical_not(early_spot)
    keyed = orders + jnp.where(pushed, TOK_DEV, 0).astype(jnp.int32)
    ranks = jnp.argsort(jnp.argsort(keyed, axis=1, stable=True), axis=1, stable=True)
    start_count = jnp.where((block_index == 1) | (block_index == 2), 0, CAP).astype(jnp.int32)
    flags = (ranks < start_count[:, None]).astype(jnp.int32)
    flags = jnp.concatenate([jnp.zeros((block_total, 1), jnp.int32), flags], axis=1).reshape(SEQ)
    return jnp.cumsum(flags).astype(jnp.int32)


def pair_draw(key):
    segment_index = segment_draw(key)
    base = jax.random.fold_in(key, 7)
    query_key, key_key, shared_key = jax.random.split(base, 3)
    shared_table = 0.7 * jax.random.normal(shared_key, (CAP * (SEQ // TOK_DEV) + 1, H * HD), jnp.float32)
    common = shared_table[segment_index]
    keys_drawn = jnp.clip(jax.random.normal(key_key, (SEQ, H * HD), jnp.float32) + common, -6.0, 6.0)
    queries_drawn = jnp.clip(jax.random.normal(query_key, (SEQ, H * HD), jnp.float32) + common, -6.0, 6.0)
    return (queries_drawn, keys_drawn)


def draw_k_raw(key, part):
    return pair_draw(key)[1].astype(jnp.bfloat16)


def draw_q_raw(key, part):
    queries_drawn, keys_drawn = pair_draw(key)
    return queries_drawn.astype(jnp.bfloat16)


def draw_v_raw(key, part):
    base = jax.random.fold_in(key, 13)
    noise_key, offset_key = jax.random.split(base)
    offsets = 0.8 * jax.random.normal(offset_key, (SEQ // BLK, H * HD), jnp.float32)
    values_drawn = jax.random.normal(noise_key, (SEQ, H * HD), jnp.float32) + jnp.repeat(offsets, BLK, axis=0)
    return jnp.clip(values_drawn, -6.0, 6.0).astype(jnp.bfloat16)


def draw_segment_ids(key, part):
    return segment_draw(key)


def level_of(own_key, extent, cuts, least, high):
    level, own = 1.0, jax.random.fold_in(own_key, 6)
    for position, shards_of in cuts:
        draws = jnp.exp(jax.random.uniform(jax.random.fold_in(own, position), (shards_of,), jnp.float32, least / len(cuts), high / len(cuts)))
        level = level * jnp.repeat(draws, extent[position] // shards_of).reshape([-1 if axis == position else 1 for axis in range(len(extent))])
    return level


def setup_inputs(seed: int = 0) -> dict:
    splits = jax.random.split(jax.random.key(seed), 7)
    return {
        "q_raw": draw_q_raw(jax.random.fold_in(splits[6], 71), 0),
        "k_raw": draw_k_raw(jax.random.fold_in(splits[6], 71), 0),
        "v_raw": draw_v_raw(jax.random.fold_in(splits[6], 71), 0),
        "block_scales": jnp.clip(jnp.exp(math.log(4.0) - 2.7725887 * jax.random.uniform(splits[3], (3, SEQ // BLK, H), jnp.float32) ** level_of(splits[3], (3, SEQ // BLK, H), ((1, 8), (2, 4)), -0.2, 0.2)), 0.25, 4.0),
        "segment_ids": draw_segment_ids(jax.random.fold_in(splits[6], 71), 0),
        "norm_gain": jnp.clip(1.0 + 0.1 * jax.random.normal(splits[5], (H * HD,), jnp.float32), 0.5, 1.5),
    }


epsilon = 1e-06

def seg_add(left, right):
    left_flag, left_value = left
    right_flag, right_value = right
    return (jnp.maximum(left_flag, right_flag), right_value + (1.0 - right_flag) * left_value)

def reference(q_raw, k_raw, v_raw, block_scales, segment_ids, norm_gain):
    seg_total = CAP * N_SEQ + 1
    half_len = TOK_DEV // 2
    block_count = SEQ // half_len
    score_scale = 1.0 / HD ** 0.5
    positions = jnp.arange(SEQ, dtype=jnp.int32)
    unit_weights = jnp.ones((SEQ, 1), jnp.float32)
    seg_counts = jax.ops.segment_sum(jnp.ones((SEQ,), jnp.float32), segment_ids, num_segments=seg_total)
    seg_size = jnp.maximum(seg_counts, 1.0)
    seg_bias = jnp.log(seg_size)
    start_flags = jnp.concatenate([jnp.ones((1, 1), jnp.float32), (segment_ids[1:] != segment_ids[:-1]).astype(jnp.float32)[:, None]], axis=0)
    run_count = lax.associative_scan(seg_add, (start_flags, unit_weights))[1][:, 0]
    block_index = positions // half_len
    edge_index = jnp.maximum((block_index - 1) * half_len - 1, 0).astype(jnp.int32)
    run_live = (block_index >= 1) & (segment_ids[edge_index] == segment_ids)
    run_total = jnp.where(run_live, run_count[edge_index], 0.0)
    run_size = jnp.maximum(run_total, 1.0)
    seg_order = jnp.arange(seg_total, dtype=jnp.int32)
    pad_ids = jnp.concatenate([jnp.full((half_len,), -1, jnp.int32), segment_ids])

    def one_head(head_index):

        def dequantize(raw, which):
            piece = lax.dynamic_slice_in_dim(raw, head_index * HD, HD, 1).astype(jnp.float32)
            factor = jnp.repeat(block_scales[which, :, head_index], BLK)[:, None]
            return (piece * factor).astype(jnp.bfloat16)
        head_query = dequantize(q_raw, 0)
        head_key = dequantize(k_raw, 1)
        head_value = dequantize(v_raw, 2)
        key_float = head_key.astype(jnp.float32)
        value_float = head_value.astype(jnp.float32)
        land_key = (jax.ops.segment_sum(key_float, segment_ids, num_segments=seg_total) / seg_size[:, None]).astype(jnp.bfloat16)
        land_value = (jax.ops.segment_sum(value_float, segment_ids, num_segments=seg_total) / seg_size[:, None]).astype(jnp.bfloat16)
        run_key = lax.associative_scan(seg_add, (start_flags, key_float))[1]
        run_value = lax.associative_scan(seg_add, (start_flags, value_float))[1]
        run_key = jnp.where(run_live[:, None], run_key[edge_index], 0.0) / run_size[:, None]
        run_value = jnp.where(run_live[:, None], run_value[edge_index], 0.0) / run_size[:, None]
        pad_key = jnp.concatenate([jnp.zeros((half_len, HD), jnp.bfloat16), head_key], axis=0)
        pad_value = jnp.concatenate([jnp.zeros((half_len, HD), jnp.bfloat16), head_value], axis=0)

        def one_block(block):
            row_start = (block * half_len).astype(jnp.int32)
            query_rows = lax.dynamic_slice_in_dim(head_query, row_start, half_len, 0)
            query_ids = lax.dynamic_slice_in_dim(segment_ids, row_start, half_len, 0)
            key_rows = lax.dynamic_slice_in_dim(pad_key, row_start, 2 * half_len, 0)
            value_rows = lax.dynamic_slice_in_dim(pad_value, row_start, 2 * half_len, 0)
            key_ids = lax.dynamic_slice_in_dim(pad_ids, row_start, 2 * half_len, 0)
            query_pos = row_start + jnp.arange(half_len, dtype=jnp.int32)
            key_pos = row_start - half_len + jnp.arange(2 * half_len, dtype=jnp.int32)
            win_mask = (key_ids[None, :] == query_ids[:, None]) & (key_pos[None, :] <= query_pos[:, None])
            win_score = jnp.dot(query_rows, key_rows.T, preferred_element_type=jnp.float32) * score_scale
            win_score = jnp.where(win_mask, win_score, -jnp.inf)
            land_score = jnp.dot(query_rows, land_key.T, preferred_element_type=jnp.float32) * score_scale + seg_bias[None, :]
            land_score = jnp.where(seg_order[None, :] < query_ids[:, None], land_score, -jnp.inf)
            live_rows = lax.dynamic_slice_in_dim(run_live, row_start, half_len, 0)
            rows_key = lax.dynamic_slice_in_dim(run_key, row_start, half_len, 0)
            rows_value = lax.dynamic_slice_in_dim(run_value, row_start, half_len, 0)
            rows_size = lax.dynamic_slice_in_dim(run_size, row_start, half_len, 0)
            run_score = lax.optimization_barrier(jnp.sum(query_rows.astype(jnp.float32) * rows_key, axis=1)) * score_scale + jnp.log(rows_size)
            run_score = jnp.where(live_rows, run_score, -jnp.inf)
            row_max = jnp.maximum(jnp.maximum(lax.optimization_barrier(jnp.max(win_score, axis=1)), lax.optimization_barrier(jnp.max(land_score, axis=1))), run_score)
            win_weight = jnp.exp(win_score - row_max[:, None])
            land_weight = jnp.exp(land_score - row_max[:, None])
            run_weight = jnp.exp(run_score - row_max)
            row_total = lax.optimization_barrier(jnp.sum(win_weight, axis=1)) + lax.optimization_barrier(jnp.sum(land_weight, axis=1)) + run_weight
            weighted = jnp.dot(win_weight.astype(jnp.bfloat16), value_rows, preferred_element_type=jnp.float32)
            weighted = weighted + jnp.dot(land_weight.astype(jnp.bfloat16), land_value, preferred_element_type=jnp.float32)
            weighted = weighted + run_weight[:, None] * rows_value
            return weighted / row_total[:, None]
        blocks = lax.map(one_block, jnp.arange(block_count, dtype=jnp.int32))
        return blocks.reshape(SEQ, HD)
    attention = lax.map(one_head, jnp.arange(H, dtype=jnp.int32))
    mean_square = lax.optimization_barrier(jnp.sum(attention * attention, axis=(0, 2))) / (H * HD)
    scaled = attention * lax.rsqrt(mean_square + epsilon)[None, :, None]
    return (jnp.transpose(scaled, (1, 0, 2)).reshape(SEQ, H * HD) * norm_gain[None, :]).astype(jnp.bfloat16)
```

```python
import functools
import math

import jax
import jax.numpy as jnp
from jax import lax
from jax.experimental import pallas as pl
from jax.experimental.pallas import tpu as pltpu
from jax.sharding import PartitionSpec as P

HD = 128
CAP = 4
LANES = 128
ROWS = 16
EARLY = CAP + 1
epsilon = 1e-06
log_two_e = math.log2(math.e)
heads_per_step = 2
f32 = jnp.float32
bf16 = jnp.bfloat16


def nt_dot(a, b):
    return lax.dot_general(a, b, (((1,), (1,)), ((), ())), preferred_element_type=f32)


def dequantized(ref, scales, which, head, cols, rows_per_scale, first_scale=0):
    parts = []
    for piece in range(ref.shape[0] // rows_per_scale):
        rows = slice(piece * rows_per_scale, (piece + 1) * rows_per_scale)
        parts.append(
            (ref[rows, cols].astype(f32) * scales[which, first_scale + piece, head]).astype(bf16)
        )
    return jnp.concatenate(parts, axis=0)


def columns_of(row):
    pieces = []
    for start in range(0, row.shape[1], LANES):
        piece = jnp.broadcast_to(row[:, start : start + LANES], (LANES, LANES))
        pieces.append(piece.T)
    return jnp.concatenate(pieces, axis=0)


def tail_kernel(which, scale_rows, scales, raw, out):
    step = pl.program_id(0)
    heads = raw.shape[1] // HD
    first = scales.shape[1] - raw.shape[0] // scale_rows
    for local in range(heads):
        cols = slice(local * HD, (local + 1) * HD)
        out[:, cols] = dequantized(
            raw, scales, which, step * heads + local, cols, scale_rows, first
        )


def table_kernel(scale_rows, scales, ids, k_raw, v_raw, table):
    step = pl.program_id(0)
    steps = pl.num_programs(0) - 1
    tokens = ids.shape[1]
    heads = k_raw.shape[1] // HD
    row = ids[...]
    local = row - row[:, 0:1]
    last = local[:, tokens - 1 :]
    slot = lax.broadcasted_iota(jnp.int32, (ROWS, tokens), 0)
    token = lax.broadcasted_iota(jnp.int32, (ROWS, tokens), 1)

    def picked(first_row):
        index = slot - first_row
        whole = (index >= 0) & (index <= CAP) & (local == index)
        early = (index == EARLY) & (local == last) & (token < tokens // 2)
        return (whole | early).astype(f32)

    pick_key, pick_value = picked(0), picked(ROWS // 2)

    @pl.when(step < steps)
    def _():
        for head in range(heads):
            cols = slice(head * HD, (head + 1) * HD)
            key = dequantized(k_raw, scales, 1, step * heads + head, cols, scale_rows)
            value = dequantized(v_raw, scales, 2, step * heads + head, cols, scale_rows)
            sums = jnp.dot(pick_key.astype(bf16), key, preferred_element_type=f32)
            sums = sums + jnp.dot(pick_value.astype(bf16), value, preferred_element_type=f32)
            table[:, :, cols] = jnp.broadcast_to(
                sums.astype(bf16)[None], (table.shape[0], ROWS, HD)
            )

    @pl.when(step == steps)
    def _():
        count = jnp.sum(pick_key + pick_value, axis=1, keepdims=True).astype(jnp.int32)
        index = lax.broadcasted_iota(jnp.int32, (ROWS, 1), 0) & (ROWS // 2 - 1)
        seg = row[:, 0:1] + jnp.where(index == EARLY, last, index)
        lane = lax.broadcasted_iota(jnp.int32, (ROWS, LANES), 1)
        meta = jnp.where(lane == 0, seg & 127, 0)
        meta = jnp.where(lane == 1, seg >> 7, meta)
        meta = jnp.where(lane == 2, count & 127, meta)
        meta = jnp.where(lane == 3, count >> 7, meta)
        meta = meta.astype(f32).astype(bf16)
        table[:, :, 0:LANES] = jnp.broadcast_to(meta[None], (table.shape[0], ROWS, LANES))


def local_kernel(scale_rows, scales, ids, q_raw, k_raw, v_raw, out, stats, near, far):
    step = pl.program_id(0)
    tokens = ids.shape[1]
    half = tokens // 2
    heads = q_raw.shape[1] // HD
    factor = log_two_e / math.sqrt(HD)

    @pl.when(step == 0)
    def _():
        row = ids[...]
        column = columns_of(row)
        for mask, start, width in ((near, 0, half), (far, half, tokens)):
            query = lax.broadcasted_iota(jnp.int32, (half, LANES), 0) + start
            for left in range(0, width, LANES):
                key = lax.broadcasted_iota(jnp.int32, (half, LANES), 1) + left
                live = (column[start : start + half] == row[:, left : left + LANES]) & (
                    key <= query
                )
                mask[:, left : left + LANES] = jnp.where(live, 0.0, -jnp.inf)

    lane = lax.broadcasted_iota(jnp.int32, (half, LANES), 1)
    for head in range(heads):
        cols = slice(head * HD, (head + 1) * HD)
        index = step * heads + head
        query = dequantized(q_raw, scales, 0, index, cols, scale_rows)
        key = dequantized(k_raw, scales, 1, index, cols, scale_rows)
        value = dequantized(v_raw, scales, 2, index, cols, scale_rows)
        for mask, start, width in ((near, 0, half), (far, half, tokens)):
            rows = slice(start, start + half)
            score = nt_dot(query[rows], key[:width]) * factor + mask[...]
            top = jnp.max(score, axis=1, keepdims=True)
            weight = jnp.exp2(score - top)
            total = jnp.sum(weight, axis=1, keepdims=True)
            out[rows, cols] = jnp.dot(
                weight.astype(bf16), value[:width], preferred_element_type=f32
            )
            kept = jnp.where(lane == 2 * head, top, total)
            if head == 0:
                stats[0, rows, :] = kept
            else:
                stats[0, rows, :] = jnp.where(lane >= 2 * head, kept, stats[0, rows, :])


def final_kernel(
    scale_rows, device_count,
    place, scales, ids, q_raw, local, stats, prev_key, prev_value, table, meta,
    out, squares,
    pick_key, pick_value, inverse, land_mask, prev_mask, power,
):
    step = pl.program_id(0)
    tokens = ids.shape[1]
    half = tokens // 2
    heads = q_raw.shape[1] // HD
    factor = log_two_e / math.sqrt(HD)
    land_total = CAP * device_count
    land_pad, entries = pick_key.shape

    @pl.when(step == 0)
    def _():
        me = place[0]
        row = ids[...]
        first = row[:, 0:1]
        column = columns_of(row)
        info = meta[...].astype(f32).T
        seg = info[0:1] + 128.0 * info[1:2]
        entry = lax.broadcasted_iota(jnp.int32, (1, entries), 1)
        device = entry // ROWS
        slot = entry & (ROWS - 1)
        is_key = slot < ROWS // 2
        slot = slot & (ROWS // 2 - 1)
        open_here = seg == first.astype(f32)
        whole = slot <= CAP
        later = open_here & whole & (device < me)
        early = (open_here & whole & (device < me - 1)) | ((slot == EARLY) & (device == me - 1))
        before = open_here & whole & (device == me - 1)
        land = lax.broadcasted_iota(jnp.int32, (land_pad, entries), 0)
        picked = (land < land_total) & (land.astype(f32) == seg) & whole
        picked = picked | ((land == land_total) & early)
        picked = picked | ((land == land_total + 1) & later)
        picked = picked | ((land == land_total + 2) & before)
        for_key = (picked & is_key).astype(f32).astype(bf16)
        pick_key[...] = for_key
        pick_value[...] = (picked & ~is_key).astype(f32).astype(bf16)
        found = jnp.dot(for_key, meta[...], preferred_element_type=f32)
        count = found[:, 2:3] + 128.0 * found[:, 3:4]
        inverse[...] = jnp.broadcast_to(1.0 / jnp.maximum(count, 1.0), inverse.shape)
        counts = nt_dot(info[0:8].astype(bf16), for_key)
        counts = counts[2:3] + 128.0 * counts[3:4]
        bias = jnp.log2(jnp.maximum(counts, 1.0))
        query = lax.broadcasted_iota(jnp.int32, (tokens, LANES), 0)
        opened = column == first
        for left in range(0, land_pad, LANES):
            cols = slice(left, left + LANES)
            lane = lax.broadcasted_iota(jnp.int32, (tokens, LANES), 1) + left
            run = jnp.where(query < half, land_total, land_total + 1)
            live = ((lane < land_total) & (lane < column)) | (
                (lane == run) & opened & (counts[:, cols] > 0.5)
            )
            land_mask[:, cols] = jnp.where(live, bias[:, cols], -jnp.inf)
        tail = counts[:, land_total + 2 : land_total + 3].astype(jnp.int32)
        for left in range(0, half, LANES):
            key = lax.broadcasted_iota(jnp.int32, (half, LANES), 1) + left
            live = (key >= half - tail) & opened[:half]
            prev_mask[:, left : left + LANES] = jnp.where(live, 0.0, -jnp.inf)

    for head in range(heads):
        cols = slice(head * HD, (head + 1) * HD)
        query = dequantized(q_raw, scales, 0, step * heads + head, cols, scale_rows)
        sums = table[:, cols]
        land_key = (
            jnp.dot(pick_key[...], sums, preferred_element_type=f32) * inverse[...]
        ).astype(bf16)
        land_value = (
            jnp.dot(pick_value[...], sums, preferred_element_type=f32) * inverse[...]
        ).astype(bf16)
        for start in (0, half):
            rows = slice(start, start + half)
            top = stats[0, rows, 2 * head : 2 * head + 1]
            total = stats[0, rows, 2 * head + 1 : 2 * head + 2]
            score = nt_dot(query[rows], land_key) * factor + land_mask[rows, :]
            new_top = jnp.maximum(top, jnp.max(score, axis=1, keepdims=True))
            if start == 0:
                prev = nt_dot(query[rows], prev_key[:, cols]) * factor + prev_mask[...]
                new_top = jnp.maximum(new_top, jnp.max(prev, axis=1, keepdims=True))
            shrink = jnp.exp2(top - new_top)
            weight = jnp.exp2(score - new_top)
            total = total * shrink + jnp.sum(weight, axis=1, keepdims=True)
            value = local[rows, cols] * shrink
            value = value + jnp.dot(weight.astype(bf16), land_value, preferred_element_type=f32)
            if start == 0:
                weight = jnp.exp2(prev - new_top)
                total = total + jnp.sum(weight, axis=1, keepdims=True)
                value = value + jnp.dot(
                    weight.astype(bf16), prev_value[:, cols], preferred_element_type=f32
                )
            value = value / total
            out[rows, cols] = value
            if head == 0:
                square = jnp.where(step == 0, 0.0, power[rows, :]) + value * value
            else:
                square = power[rows, :] + value * value
            power[rows, :] = square

    @pl.when(step == pl.num_programs(0) - 1)
    def _():
        ones = jnp.ones((8, LANES), f32)
        squares[...] = lax.dot_general(
            ones, power[...], (((1,), (1,)), ((), ())),
            precision=lax.Precision.HIGHEST, preferred_element_type=f32,
        )[0:1]


def scale_kernel(width, count, *refs):
    squares, (gain, raw, out) = refs[:count], refs[count:]
    total = squares[0][...]
    for ref in squares[1:]:
        total = total + ref[...]
    norm = lax.rsqrt(total / width + epsilon)
    norm = columns_of(norm)
    for left in range(0, raw.shape[1], LANES):
        cols = slice(left, left + LANES)
        out[:, cols] = (raw[:, cols] * norm * gain[:, cols]).astype(out.dtype)


def on_device(q_raw, k_raw, v_raw, block_scales, segment_ids, norm_gain):
    tokens, width = q_raw.shape
    half = tokens // 2
    scale_rows = tokens // block_scales.shape[1]
    devices = lax.axis_size("seq")
    head_devices = lax.axis_size("head")
    step_width = heads_per_step * HD
    steps = width // step_width
    entries = devices * ROWS
    land_pad = -(-(CAP * devices + 3) // LANES) * LANES
    smem = pl.BlockSpec(memory_space=pltpu.SMEM)
    sds = jax.ShapeDtypeStruct
    ids = segment_ids.reshape(1, tokens)
    ids_spec = pl.BlockSpec((1, tokens), lambda s: (0, 0))
    full_rows = pl.BlockSpec((tokens, step_width), lambda s: (0, s))
    half_rows = pl.BlockSpec((half, step_width), lambda s: (0, s))

    def tails(raw, which):
        return pl.pallas_call(
            functools.partial(tail_kernel, which, scale_rows),
            name="tail_%d" % which,
            grid=(2,),
            in_specs=[smem, pl.BlockSpec((half, width // 2), lambda s: (1, s))],
            out_specs=pl.BlockSpec((half, width // 2), lambda s: (0, s)),
            out_shape=sds((half, width), bf16),
            cost_estimate=pl.CostEstimate(flops=half * width, bytes_accessed=4 * half * width, transcendentals=0),
        )(block_scales, raw)

    def shifted(block):
        return lax.ppermute(block, "seq", [(i - 1, i) for i in range(1, devices)])

    prev_key = shifted(tails(k_raw, 1))
    prev_value = shifted(tails(v_raw, 2))

    table_steps = 4
    table_width = width // table_steps
    last = table_steps - 1
    clipped = pl.BlockSpec((tokens, table_width), lambda s: (0, jnp.minimum(s, last)))
    table = pl.pallas_call(
        functools.partial(table_kernel, scale_rows),
        name="table",
        grid=(table_steps + 1,),
        in_specs=[smem, ids_spec, clipped, clipped],
        out_specs=pl.BlockSpec((devices, ROWS, table_width), lambda s: (0, 0, s)),
        out_shape=sds((devices, ROWS, width + LANES), bf16),
        cost_estimate=pl.CostEstimate(flops=64 * tokens * width, bytes_accessed=4 * tokens * width, transcendentals=0),
    )(block_scales, ids, k_raw, v_raw)
    table = lax.all_to_all(table, "seq", 0, 0, tiled=True).reshape(entries, width + LANES)

    attended, stats = pl.pallas_call(
        functools.partial(local_kernel, scale_rows),
        name="local",
        grid=(steps,),
        in_specs=[smem, ids_spec, full_rows, full_rows, full_rows],
        out_specs=[full_rows, pl.BlockSpec((1, tokens, LANES), lambda s: (s, 0, 0))],
        out_shape=[sds((tokens, width), f32), sds((steps, tokens, LANES), f32)],
        scratch_shapes=[pltpu.VMEM((half, half), f32), pltpu.VMEM((half, tokens), f32)],
        cost_estimate=pl.CostEstimate(
            flops=3 * half * tokens * width * 2, bytes_accessed=10 * tokens * width, transcendentals=half * tokens * 12
        ),
    )(block_scales, ids, q_raw, k_raw, v_raw)

    place = lax.axis_index("seq").astype(jnp.int32).reshape(1)
    attended, squares = pl.pallas_call(
        functools.partial(final_kernel, scale_rows, devices),
        name="final",
        grid=(steps,),
        in_specs=[
            smem, smem, ids_spec, full_rows, full_rows,
            pl.BlockSpec((1, tokens, LANES), lambda s: (s, 0, 0)),
            half_rows, half_rows,
            pl.BlockSpec((entries, step_width), lambda s: (0, s)),
            pl.BlockSpec((entries, LANES), lambda s: (0, width // LANES)),
        ],
        out_specs=[full_rows, pl.BlockSpec((1, tokens), lambda s: (0, 0))],
        out_shape=[sds((tokens, width), f32), sds((1, tokens), f32)],
        scratch_shapes=[
            pltpu.VMEM((land_pad, entries), bf16),
            pltpu.VMEM((land_pad, entries), bf16),
            pltpu.VMEM((land_pad, LANES), f32),
            pltpu.VMEM((tokens, land_pad), f32),
            pltpu.VMEM((half, half), f32),
            pltpu.VMEM((tokens, LANES), f32),
        ],
        cost_estimate=pl.CostEstimate(
            flops=2 * half * tokens * width * 2, bytes_accessed=14 * tokens * width, transcendentals=half * tokens * 8
        ),
    )(place, block_scales, ids, q_raw, attended, stats, prev_key, prev_value, table, table)

    parts = [squares] + [
        lax.ppermute(squares, "head", [(i, (i + d) % head_devices) for i in range(head_devices)])
        for d in range(1, head_devices)
    ]
    rows_out = tokens // 4
    part_spec = pl.BlockSpec((1, rows_out), lambda s: (0, s))
    row_spec = pl.BlockSpec((rows_out, width), lambda s: (s, 0))
    return pl.pallas_call(
        functools.partial(scale_kernel, width * head_devices, head_devices),
        name="scale",
        grid=(4,),
        in_specs=[part_spec] * head_devices + [pl.BlockSpec((1, width), lambda s: (0, 0)), row_spec],
        out_specs=row_spec,
        out_shape=sds((tokens, width), bf16),
        cost_estimate=pl.CostEstimate(flops=3 * tokens * width, bytes_accessed=6 * tokens * width, transcendentals=tokens),
    )(*parts, norm_gain.reshape(1, width), attended)


def solution(mesh):
    in_specs = (
        P("seq", "head"), P("seq", "head"), P("seq", "head"),
        P(None, "seq", "head"), P("seq"), P("head"),
    )
    return jax.shard_map(
        on_device, mesh=mesh, in_specs=in_specs, out_specs=P("seq", "head"), check_vma=False
    )
```

```python
import functools
import math

import jax
import jax.numpy as jnp
from jax import lax
from jax.experimental import pallas as pl
from jax.experimental.pallas import tpu as pltpu
from jax.sharding import PartitionSpec as P

HD = 128
CAP = 4
LANES = 128
SLOTS = CAP + 2
EARLY = CAP + 1
epsilon = 1e-06
factor = math.log2(math.e) / math.sqrt(HD)
f32 = jnp.float32
bf16 = jnp.bfloat16
i32 = jnp.int32
vmem_limit = 20 * 2**20


def nt_dot(a, b):
    return lax.dot_general(a, b, (((1,), (1,)), ((), ())), preferred_element_type=f32)


def nn_dot(a, b):
    return jnp.dot(a, b, preferred_element_type=f32)


def iota(shape, axis):
    return lax.broadcasted_iota(i32, shape, axis)


def columns_of(row):
    pieces = []
    for start in range(0, row.shape[1], LANES):
        pieces.append(jnp.broadcast_to(row[:, start : start + LANES], (LANES, LANES)).T)
    return jnp.concatenate(pieces, axis=0)


def head_cols(head):
    return pl.ds(pl.multiple_of(head * HD, HD), HD)


def dequantized(raw, scales, which, head, first, cols, scale_rows):
    parts = []
    for piece in range(raw.shape[0] // scale_rows):
        rows = slice(piece * scale_rows, (piece + 1) * scale_rows)
        parts.append((raw[rows, cols].astype(f32) * scales[which, first + piece, head]).astype(bf16))
    return jnp.concatenate(parts, axis=0)


def tail_kernel(scale_rows, scales, raw, out):
    first = scales.shape[1] - raw.shape[0] // scale_rows
    for head in range(raw.shape[1] // HD):
        cols = slice(head * HD, (head + 1) * HD)
        out[:, cols] = dequantized(raw, scales, 1, head, first, cols, scale_rows)


def table_kernel(scale_rows, scales, ids, k_raw, tail_key, v_raw, table, front_key, front_value, tail_value, sums):
    tokens = ids.shape[1]
    half = tokens // 2
    heads = v_raw.shape[1] // HD
    row = ids[...]
    local = row - row[:, 0:1]
    last = local[:, tokens - 1 :]
    slot = iota((2 * 8, tokens), 0)
    token = iota((2 * 8, tokens), 1)
    picked = (slot <= CAP) & (local == slot)
    picked = picked | ((slot == EARLY) & (local == last) & (token < half))
    picked = picked.astype(f32)
    pick = picked.astype(bf16)
    for head in range(heads):
        cols = slice(head * HD, (head + 1) * HD)
        front = dequantized(k_raw, scales, 1, head, 0, cols, scale_rows)
        front_key[:, cols] = front
        found = nn_dot(pick[:, :half], front) + nn_dot(pick[:, half:], tail_key[:, cols])
        for index in range(SLOTS):
            sums[head : head + 1, index * HD : (index + 1) * HD] = found[index : index + 1]
        value = dequantized(v_raw, scales, 2, head, 0, cols, scale_rows)
        front_value[cols, :] = value[:half].T
        tail_value[cols, :] = value[half:].T
        found = nn_dot(pick, value)
        for index in range(SLOTS):
            sums[head : head + 1, (SLOTS + index) * HD : (SLOTS + index + 1) * HD] = found[index : index + 1]
    count = jnp.sum(picked, axis=1, keepdims=True).astype(i32)
    lane = iota((heads, LANES), 1)
    meta = jnp.zeros((heads, LANES), i32)
    for index in range(SLOTS):
        seg = row[:, 0:1] + (last if index == EARLY else index)
        number = count[index : index + 1]
        for place, value in enumerate((seg & 127, seg >> 7, number & 127, number >> 7)):
            meta = jnp.where(lane == 4 * index + place, value, meta)
    sums[:, 2 * SLOTS * HD :] = meta.astype(f32)
    table[...] = jnp.broadcast_to(sums[...].astype(bf16)[None], table.shape)


def with_ones(value):
    return jnp.concatenate([value, jnp.ones((16, value.shape[1]), bf16)], axis=0)


def local_kernel(
    scale_rows, scales, ids, q_raw, front_key, tail_key, front_value, tail_value,
    query_out, out, tops, totals, near, far,
):
    tokens = ids.shape[1]
    half = tokens // 2
    heads = q_raw.shape[1] // HD
    row = ids[...]
    column = columns_of(row)
    for mask, start, width in ((near, 0, half), (far, half, tokens)):
        for left in range(0, half, LANES):
            query = iota((width, LANES), 1) + (start + left)
            live = column[:width] == row[:, start + left : start + left + LANES]
            live = live & (iota((width, LANES), 0) <= query)
            mask[:, left : left + LANES] = jnp.where(live, 0.0, -jnp.inf)

    def one_head(head):
        cols = head_cols(head)
        query = dequantized(q_raw, scales, 0, head, 0, cols, scale_rows)
        query_out[:, cols] = query
        scores = (
            nt_dot(front_key[:, cols], query[:half]) * factor + near[...],
            nt_dot(jnp.concatenate([front_key[:, cols], tail_key[:, cols]], axis=0), query[half:]) * factor + far[...],
        )
        values = (
            front_value[cols, :],
            jnp.concatenate([front_value[cols, :], tail_value[cols, :]], axis=1),
        )
        for part in range(2):
            where = slice(part * half, (part + 1) * half)
            top = jnp.max(scores[part], axis=0, keepdims=True)
            weight = jnp.exp2(scores[part] - top).astype(bf16)
            found = nn_dot(with_ones(values[part]), weight)
            out[cols, where] = found[:HD]
            tops[pl.ds(head, 1), where] = top
            totals[pl.ds(head, 1), where] = found[HD : HD + 1]

    def body(pair, carry):
        one_head(2 * pair)
        one_head(2 * pair + 1)
        return carry

    lax.fori_loop(0, heads // 2, body, 0)


def landmark_kernel(
    device_count,
    place, ids, query, local, tops, totals, table,
    open_out, open_tops, open_totals, done_out, done_squares, prev_mask,
    picks, bias,
):
    tokens = ids.shape[1]
    half = tokens // 2
    heads = query.shape[1] // HD
    lands = CAP * device_count
    land_pad, entries = picks.shape[1:]
    me = place[0]
    row = ids[...]
    first = row[:, 0:1]
    info = table[:, 2 * SLOTS * HD :].astype(f32).T
    entry = iota((1, entries), 1)
    device = entry // heads
    entry_head = entry - device * heads
    land = iota((land_pad, entries), 0)
    count = jnp.zeros((land_pad, 1), f32)
    for index in range(SLOTS):
        seg = info[4 * index : 4 * index + 1] + 128.0 * info[4 * index + 1 : 4 * index + 2]
        number = info[4 * index + 2 : 4 * index + 3] + 128.0 * info[4 * index + 3 : 4 * index + 4]
        if index == EARLY:
            picked = (land == lands) & (device == me - 1)
        else:
            is_open = seg == first.astype(f32)
            picked = (land < lands) & (land.astype(f32) == seg)
            picked = picked | ((land == lands) & is_open & (device < me - 1))
            picked = picked | ((land == lands + 1) & is_open & (device < me))
            picked = picked | ((land == lands + 2) & is_open & (device == me - 1))
        picked = picked.astype(f32)
        picks[index] = picked.astype(bf16)
        count = count + jnp.sum(
            picked * jnp.where(entry_head == 0, number, 0.0), axis=1, keepdims=True
        )
    inverse = jnp.broadcast_to(1.0 / jnp.maximum(count, 1.0), (land_pad, HD))
    amount = jnp.broadcast_to(count, (land_pad, LANES))
    log_count = jnp.log2(jnp.maximum(amount, 1.0))
    for left in range(0, tokens, LANES):
        seg = row[:, left : left + LANES]
        index = iota((land_pad, LANES), 0)
        run = lands if left < half else lands + 1
        live = ((index < lands) & (index < seg)) | ((index == run) & (seg == first) & (amount > 0.5))
        bias[:, left : left + LANES] = jnp.where(live, log_count, -jnp.inf)
    tail = count[lands + 2 : lands + 3].astype(i32)
    for left in range(0, half, LANES):
        live = (iota((half, LANES), 0) >= half - tail) & (row[:, left : left + LANES] == first)
        prev_mask[:, left : left + LANES] = jnp.where(live, 0.0, -jnp.inf)

    def one_head(head):
        cols = head_cols(head)
        mine = (entry_head == head).astype(f32).astype(bf16)
        key = jnp.zeros((land_pad, HD), f32)
        value = jnp.zeros((land_pad, HD), f32)
        for index in range(SLOTS):
            pick = picks[index] * mine
            key = key + nn_dot(pick, table[:, index * HD : (index + 1) * HD])
            value = value + nn_dot(pick, table[:, (SLOTS + index) * HD : (SLOTS + index + 1) * HD])
        key = (key * inverse).astype(bf16)
        value = (value * inverse).astype(bf16)
        value = jnp.concatenate([value, jnp.ones((land_pad, 16), bf16)], axis=1)
        score = nt_dot(key, query[:, cols]) * factor + bias[...]
        top = tops[pl.ds(head, 1), :]
        new_top = jnp.maximum(top, jnp.max(score, axis=0, keepdims=True))
        shrink = jnp.exp2(top - new_top)
        weight = jnp.exp2(score - new_top).astype(bf16)
        found = lax.dot_general(value, weight, (((0,), (0,)), ((), ())), preferred_element_type=f32)
        total = totals[pl.ds(head, 1), :] * shrink + found[HD : HD + 1]
        found = local[cols, :] * shrink + found[:HD]
        open_tops[pl.ds(head, 1), :] = new_top[:, :half]
        open_totals[pl.ds(head, 1), :] = total[:, :half]
        open_out[cols, :] = found[:, :half]
        done = found[:, half:] * (1.0 / total[:, half:])
        done_out[cols, :] = done
        return jnp.sum(done * done, axis=0, keepdims=True)

    def body(pair, squares):
        return squares + one_head(2 * pair) + one_head(2 * pair + 1)

    done_squares[...] = lax.fori_loop(0, heads // 2, body, jnp.zeros((1, half), f32))


def halo_kernel(
    query, local, tops, totals, prev_mask, done_squares, prev_key, prev_value,
    out, squares,
):
    half = prev_mask.shape[0]
    heads = query.shape[1] // HD

    def one_head(head):
        cols = head_cols(head)
        score = nt_dot(prev_key[:, cols], query[:half, cols]) * factor + prev_mask[...]
        top = tops[pl.ds(head, 1), :]
        new_top = jnp.maximum(top, jnp.max(score, axis=0, keepdims=True))
        shrink = jnp.exp2(top - new_top)
        weight = jnp.exp2(score - new_top).astype(bf16)
        found = nn_dot(with_ones(prev_value[cols, :]), weight)
        total = totals[pl.ds(head, 1), :] * shrink + found[HD : HD + 1]
        done = (local[cols, :] * shrink + found[:HD]) * (1.0 / total)
        out[cols, :] = done
        return jnp.sum(done * done, axis=0, keepdims=True)

    def body(pair, carry):
        return carry + one_head(2 * pair) + one_head(2 * pair + 1)

    squares[:, :half] = lax.fori_loop(0, heads // 2, body, jnp.zeros((1, half), f32))
    squares[:, half:] = done_squares[...]


def scale_kernel(width, count, *refs):
    parts, (gain, front, back, out) = refs[:count], refs[count:]
    total = parts[0][...]
    for ref in parts[1:]:
        total = total + ref[...]
    norm = lax.rsqrt(total / width + epsilon)
    half = front.shape[1]
    heads = front.shape[0] // HD
    gains = columns_of(gain[...])
    for head in range(heads):
        cols = slice(head * HD, (head + 1) * HD)
        for source, start in ((front, 0), (back, half)):
            for left in range(0, half, LANES):
                rows = slice(start + left, start + left + LANES)
                value = source[cols, left : left + LANES] * norm[:, rows] * gains[cols]
                out[rows, cols] = value.astype(bf16).T


def on_device(q_raw, k_raw, v_raw, block_scales, segment_ids, norm_gain):
    tokens, width = q_raw.shape
    half = tokens // 2
    heads = width // HD
    scale_rows = tokens // block_scales.shape[1]
    devices = lax.axis_size("seq")
    head_devices = lax.axis_size("head")
    entries = devices * heads
    land_pad = -(-(CAP * devices + 3) // 16) * 16
    smem = pl.BlockSpec(memory_space=pltpu.SMEM)
    vmem = pl.BlockSpec(memory_space=pltpu.VMEM)
    sds = jax.ShapeDtypeStruct
    ids = segment_ids.reshape(1, tokens)
    wide = 2 * SLOTS * HD + LANES

    def call(kernel, name, out_shape, in_specs, args, flops, moved, scratch=(), out_specs=None, limit=vmem_limit, **more):
        return pl.pallas_call(
            kernel,
            name=name,
            out_shape=out_shape,
            in_specs=in_specs,
            out_specs=jax.tree.map(lambda _: vmem, out_shape) if out_specs is None else out_specs,
            scratch_shapes=list(scratch),
            compiler_params=pltpu.CompilerParams(vmem_limit_bytes=limit),
            cost_estimate=pl.CostEstimate(flops=flops, bytes_accessed=moved, transcendentals=0),
            **more,
        )(*args)

    def shifted(block):
        return lax.ppermute(block, "seq", [(i - 1, i) for i in range(1, devices)])

    tail_key = call(
        functools.partial(tail_kernel, scale_rows), "tail", sds((half, width), bf16),
        [smem, pl.BlockSpec((half, width), lambda s: (1, 0))], (block_scales, k_raw),
        half * width, 4 * half * width, grid=(1,), out_specs=pl.BlockSpec((half, width), lambda s: (0, 0)),
    )
    prev_key = shifted(tail_key)
    table, front_key, front_value, tail_value = call(
        functools.partial(table_kernel, scale_rows), "table",
        [sds((devices, heads, wide), bf16), sds((half, width), bf16), sds((width, half), bf16), sds((width, half), bf16)],
        [smem, pl.BlockSpec((1, tokens), lambda s: (0, 0)), pl.BlockSpec((half, width), lambda s: (0, 0)),
         pl.BlockSpec((half, width), lambda s: (0, 0)), pl.BlockSpec((tokens, width), lambda s: (0, 0))],
        (block_scales, ids, k_raw, tail_key, v_raw),
        64 * tokens * width, 4 * tokens * width, grid=(1,),
        out_specs=[
            pl.BlockSpec((devices, heads, wide), lambda s: (0, 0, 0)), pl.BlockSpec((half, width), lambda s: (0, 0)),
            pl.BlockSpec((width, half), lambda s: (0, 0)), pl.BlockSpec((width, half), lambda s: (0, 0)),
        ],
        scratch=[pltpu.VMEM((heads, wide), f32)],
    )
    table = lax.all_to_all(table, "seq", 0, 0, tiled=True).reshape(entries, wide)
    prev_value = shifted(tail_value)
    query, local, tops, totals = call(
        functools.partial(local_kernel, scale_rows), "local",
        [sds((tokens, width), bf16), sds((width, tokens), f32), sds((heads, tokens), f32), sds((heads, tokens), f32)],
        [smem] + [vmem] * 6, (block_scales, ids, q_raw, front_key, tail_key, front_value, tail_value),
        6 * half * tokens * width, 12 * tokens * width,
        scratch=[pltpu.VMEM((half, half), f32), pltpu.VMEM((tokens, half), f32)],
    )
    place = lax.axis_index("seq").astype(i32).reshape(1)
    part, tops, totals, back, back_squares, prev_mask = call(
        functools.partial(landmark_kernel, devices), "landmark",
        [sds((width, half), f32), sds((heads, half), f32), sds((heads, half), f32), sds((width, half), f32), sds((1, half), f32), sds((half, half), f32)],
        [smem] + [vmem] * 6, (place, ids, query, local, tops, totals, table),
        half * tokens * width, 12 * tokens * width,
        scratch=[pltpu.VMEM((SLOTS, land_pad, entries), bf16), pltpu.VMEM((land_pad, tokens), f32)],
    )
    front, squares = call(
        halo_kernel, "halo", [sds((width, half), f32), sds((1, tokens), f32)],
        [vmem] * 8, (query, part, tops, totals, prev_mask, back_squares, prev_key, prev_value),
        2 * half * tokens * width, 8 * tokens * width,
    )
    parts = [squares] + [
        lax.ppermute(squares, "head", [(i, (i + d) % head_devices) for i in range(head_devices)])
        for d in range(1, head_devices)
    ]
    return call(
        functools.partial(scale_kernel, width * head_devices, head_devices), "scale", sds((tokens, width), bf16),
        [vmem] * (head_devices + 3), (*parts, norm_gain.reshape(1, width), front, back),
        3 * tokens * width, 6 * tokens * width,
    )


def solution(mesh):
    in_specs = (
        P("seq", "head"), P("seq", "head"), P("seq", "head"),
        P(None, "seq", "head"), P("seq"), P("head"),
    )
    return jax.shard_map(
        on_device, mesh=mesh, in_specs=in_specs, out_specs=P("seq", "head"), check_vma=False
    )
```

```python
import functools
import math

import jax
import jax.numpy as jnp
from jax import lax
from jax.experimental import pallas as pl
from jax.experimental.pallas import tpu as pltpu
from jax.sharding import PartitionSpec as P


HD = 128
CAP = 4
LANES = 128
SLOTS = CAP + 2
EARLY = CAP + 1
epsilon = 1e-06
factor = math.log2(math.e) / math.sqrt(HD)
f32 = jnp.float32
bf16 = jnp.bfloat16
i32 = jnp.int32
vmem_limit = 20 * 2**20
whole_vmem = 60 * 1024 * 2**10
pipeline_depth = 2


def nt_dot(a, b):
    return lax.dot_general(a, b, (((1,), (1,)), ((), ())), preferred_element_type=f32)


def nn_dot(a, b):
    return jnp.dot(a, b, preferred_element_type=f32)


def iota(shape, axis):
    return lax.broadcasted_iota(i32, shape, axis)


def columns_of(row):
    pieces = []
    for start in range(0, row.shape[1], LANES):
        pieces.append(jnp.broadcast_to(row[:, start : start + LANES], (LANES, LANES)).T)
    return jnp.concatenate(pieces, axis=0)


def dequantized(raw, scales, which, head, cols, scale_rows, first=0):
    parts = []
    for piece in range(raw.shape[0] // scale_rows):
        rows = slice(piece * scale_rows, (piece + 1) * scale_rows)
        parts.append((raw[rows, cols].astype(f32) * scales[which, first + piece, head]).astype(bf16))
    return jnp.concatenate(parts, axis=0)


def tail_kernel(scale_rows, scales, raw, out):
    first = scales.shape[1] - raw.shape[0] // scale_rows
    heads = raw.shape[1] // HD
    for head in range(heads):
        cols = slice(head * HD, (head + 1) * HD)
        index = pl.program_id(0) * heads + head
        out[:, cols] = dequantized(raw, scales, 1, index, cols, scale_rows, first)


def table_kernel(scale_rows, scales, ids, k_raw, v_raw, table, tail_value, sums, parts):
    step = pl.program_id(0)
    tokens = ids.shape[1]
    half = tokens // 2
    heads = v_raw.shape[1] // HD
    all_heads = sums.shape[0]
    row = ids[...]
    local = row - row[:, 0:1]
    last = local[:, tokens - 1 :]
    slot = iota((2 * 8, tokens), 0)
    token = iota((2 * 8, tokens), 1)
    picked = (slot <= CAP) & (local == slot)
    picked = picked | ((slot == EARLY) & (local == last) & (token < half))
    picked = picked.astype(f32)
    pick = picked.astype(bf16)
    for head in range(heads):
        cols = slice(head * HD, (head + 1) * HD)
        index = step * heads + head
        key = dequantized(k_raw, scales, 1, index, cols, scale_rows)
        value = dequantized(v_raw, scales, 2, index, cols, scale_rows)
        tail_value[cols, :] = value[half:].T
        parts[index, 0] = nn_dot(pick, key)[:8]
        parts[index, 1] = nn_dot(pick, value)[:8]

    @pl.when(step == pl.num_programs(0) - 1)
    def _():
        count = jnp.sum(picked, axis=1, keepdims=True).astype(i32)
        lane = iota((all_heads, LANES), 1)
        meta = jnp.zeros((all_heads, LANES), i32)
        for index in range(SLOTS):
            seg = row[:, 0:1] + (last if index == EARLY else index)
            number = count[index : index + 1]
            for place, value in enumerate((seg & 127, seg >> 7, number & 127, number >> 7)):
                meta = jnp.where(lane == 4 * index + place, value, meta)
        for head in range(all_heads):
            for which in range(2):
                found = parts[head, which]
                for place in range(SLOTS):
                    where = slice((which * SLOTS + place) * HD, (which * SLOTS + place + 1) * HD)
                    sums[head : head + 1, where] = found[place : place + 1]
        sums[:, 2 * SLOTS * HD :] = meta.astype(f32)
        table[...] = jnp.broadcast_to(sums[...].astype(bf16)[None], table.shape)


def with_ones(value):
    return jnp.concatenate([value, jnp.ones((16, value.shape[1]), bf16)], axis=0)


def main_kernel(
    scale_rows, device_count,
    place, scales, ids, table, gain, q_raw, k_raw, v_raw,
    query_out, open_out, open_tops, open_totals, back_out, back_squares, prev_mask,
    near, far, picks, bias, inverse,
):
    step = pl.program_id(0)
    tokens = ids.shape[1]
    half = tokens // 2
    heads = q_raw.shape[1] // HD
    lands = CAP * device_count
    land_pad, entries = picks.shape[1:]
    all_heads = entries // device_count
    entry = iota((1, entries), 1)
    entry_device = entry // all_heads
    entry_head = entry - entry_device * all_heads

    @pl.when(step == 0)
    def _():
        me = place[0]
        row = ids[...]
        first = row[:, 0:1]
        column = columns_of(row)
        for mask, start, width in ((near, 0, half), (far, half, tokens)):
            for left in range(0, half, LANES):
                query = iota((width, LANES), 1) + (start + left)
                live = column[:width] == row[:, start + left : start + left + LANES]
                live = live & (iota((width, LANES), 0) <= query)
                mask[:, left : left + LANES] = jnp.where(live, 0.0, -jnp.inf)
        info = table[:, 2 * SLOTS * HD :].astype(f32).T
        land = iota((land_pad, entries), 0)
        count = jnp.zeros((land_pad, 1), f32)
        for index in range(SLOTS):
            seg = info[4 * index : 4 * index + 1] + 128.0 * info[4 * index + 1 : 4 * index + 2]
            number = info[4 * index + 2 : 4 * index + 3] + 128.0 * info[4 * index + 3 : 4 * index + 4]
            if index == EARLY:
                picked = (land == lands) & (entry_device == me - 1)
            else:
                is_open = seg == first.astype(f32)
                picked = (land < lands) & (land.astype(f32) == seg)
                picked = picked | ((land == lands) & is_open & (entry_device < me - 1))
                picked = picked | ((land == lands + 1) & is_open & (entry_device < me))
                picked = picked | ((land == lands + 2) & is_open & (entry_device == me - 1))
            picked = picked.astype(f32)
            picks[index] = picked.astype(bf16)
            count = count + jnp.sum(
                picked * jnp.where(entry_head == 0, number, 0.0), axis=1, keepdims=True
            )
        inverse[...] = jnp.broadcast_to(1.0 / jnp.maximum(count, 1.0), inverse.shape)
        amount = jnp.broadcast_to(count, (land_pad, LANES))
        log_count = jnp.log2(jnp.maximum(amount, 1.0))
        for left in range(0, tokens, LANES):
            seg = row[:, left : left + LANES]
            index = iota((land_pad, LANES), 0)
            run = lands if left < half else lands + 1
            live = ((index < lands) & (index < seg)) | ((index == run) & (seg == first) & (amount > 0.5))
            bias[:, left : left + LANES] = jnp.where(live, log_count, -jnp.inf)
        tail = count[lands + 2 : lands + 3].astype(i32)
        for left in range(0, half, LANES):
            live = (iota((half, LANES), 0) >= half - tail) & (row[:, left : left + LANES] == first)
            prev_mask[:, left : left + LANES] = jnp.where(live, 0.0, -jnp.inf)
        back_squares[...] = jnp.zeros(back_squares.shape, f32)

    def prepared(head):
        cols = slice(head * HD, (head + 1) * HD)
        index = step * heads + head
        query = dequantized(q_raw, scales, 0, index, cols, scale_rows)
        key = dequantized(k_raw, scales, 1, index, cols, scale_rows)
        value = dequantized(v_raw, scales, 2, index, cols, scale_rows).T
        query_out[:, cols] = query[:half]
        mine = (entry_head == index).astype(f32).astype(bf16)
        land_key = jnp.zeros((land_pad, HD), f32)
        land_value = jnp.zeros((land_pad, HD), f32)
        for slot in range(SLOTS):
            pick = picks[slot] * mine
            land_key = land_key + nn_dot(pick, table[:, slot * HD : (slot + 1) * HD])
            land_value = land_value + nn_dot(pick, table[:, (SLOTS + slot) * HD : (SLOTS + slot + 1) * HD])
        land_key = (land_key * inverse[...]).astype(bf16)
        land_value = (land_value * inverse[...]).astype(bf16)
        land_value = jnp.concatenate([land_value, jnp.ones((land_pad, 16), bf16)], axis=1)
        return query, key, value, land_key, land_value

    ready = {}

    def scores_of(task):
        head, part = task
        if head not in ready:
            ready[head] = prepared(head)
        query, key, _, land_key, _ = ready[head]
        rows = slice(part * half, (part + 1) * half)
        mask = far if part else near
        score = nt_dot(key[: (part + 1) * half], query[rows]) * factor + mask[...]
        return score, nt_dot(land_key, query[rows]) * factor + bias[:, rows]

    tasks = [(head, part) for head in range(heads) for part in range(2)]
    scores = [scores_of(task) for task in tasks[:pipeline_depth]]
    for number, (head, part) in enumerate(tasks):
        if number + pipeline_depth < len(tasks):
            scores.append(scores_of(tasks[number + pipeline_depth]))
        cols = slice(head * HD, (head + 1) * HD)
        score, land_score = scores[number]
        _, _, value, _, land_value = ready[head]
        top = jnp.maximum(
            jnp.max(score, axis=0, keepdims=True), jnp.max(land_score, axis=0, keepdims=True)
        )
        weight = jnp.exp2(score - top).astype(bf16)
        land_weight = jnp.exp2(land_score - top).astype(bf16)
        found = nn_dot(with_ones(value[:, : (part + 1) * half]), weight)
        found = found + lax.dot_general(
            land_value, land_weight, (((0,), (0,)), ((), ())), preferred_element_type=f32
        )
        total = found[HD : HD + 1]
        if part == 0:
            open_out[cols, :] = found[:HD]
            open_tops[0, head : head + 1, :] = top
            open_totals[0, head : head + 1, :] = total
        else:
            done = found[:HD] * (1.0 / total)
            back_squares[...] += jnp.sum(done * done, axis=0, keepdims=True)
            back_out[:, cols] = done.T * gain[:, cols]


def halo_kernel(
    query, local, tops, totals, gain, prev_mask, done_squares, prev_key, prev_value,
    out, squares,
):
    half = prev_mask.shape[0]
    heads = query.shape[1] // HD
    per_step = tops.shape[1]
    chunk = 256
    tasks = [(head, left) for head in range(heads) for left in range(0, half, chunk)]

    def score_of(task):
        head, left = task
        cols = slice(head * HD, (head + 1) * HD)
        rows = slice(left, left + chunk)
        return nt_dot(prev_key[:, cols], query[rows, cols]) * factor + prev_mask[:, rows]

    def finish(task, score):
        head, left = task
        cols = slice(head * HD, (head + 1) * HD)
        rows = slice(left, left + chunk)
        step, place = head // per_step, head % per_step
        top = tops[step, place : place + 1, rows]
        new_top = jnp.maximum(top, jnp.max(score, axis=0, keepdims=True))
        shrink = jnp.exp2(top - new_top)
        weight = jnp.exp2(score - new_top).astype(bf16)
        found = nn_dot(with_ones(prev_value[cols, :]), weight)
        total = totals[step, place : place + 1, rows] * shrink + found[HD : HD + 1]
        done = (local[cols, rows] * shrink + found[:HD]) * (1.0 / total)
        return done

    sums = [jnp.zeros((1, chunk), f32)] * (half // chunk)
    depth = 2
    scores = [score_of(task) for task in tasks[:depth]]
    for number, task in enumerate(tasks):
        if number + depth < len(tasks):
            scores.append(score_of(tasks[number + depth]))
        done = finish(task, scores[number])
        head, left = task
        sums[left // chunk] = sums[left // chunk] + jnp.sum(done * done, axis=0, keepdims=True)
        out[left : left + chunk, head * HD : (head + 1) * HD] = done.T * gain[:, head * HD : (head + 1) * HD]
    for index, found in enumerate(sums):
        squares[:, index * chunk : (index + 1) * chunk] = found
    squares[:, half:] = done_squares[...]


def scale_kernel(width, count, *refs):
    parts, (front, back, out, ready, sems) = refs[:count], refs[count:]
    total = parts[0][...]
    for ref in parts[1:]:
        total = total + ref[...]
    norm = columns_of(lax.rsqrt(total / width + epsilon))
    half = front.shape[0]
    copies = []
    for part, source in enumerate((front, back)):
        for start in range(0, half, LANES):
            rows = slice(part * half + start, part * half + start + LANES)
            for left in range(0, front.shape[1], LANES):
                cols = slice(left, left + LANES)
                ready[rows, cols] = (source[start : start + LANES, cols] * norm[rows]).astype(bf16)
            copy = pltpu.make_async_copy(ready.at[rows], out.at[rows], sems.at[len(copies)])
            copy.start()
            copies.append(copy)
    for copy in copies:
        copy.wait()


def on_device(q_raw, k_raw, v_raw, block_scales, segment_ids, norm_gain):
    tokens, width = q_raw.shape
    half = tokens // 2
    heads = width // HD
    scale_rows = tokens // block_scales.shape[1]
    devices = lax.axis_size("seq")
    head_devices = lax.axis_size("head")
    entries = devices * heads
    land_pad = -(-(CAP * devices + 3) // 16) * 16
    smem = pl.BlockSpec(memory_space=pltpu.SMEM)
    vmem = pl.BlockSpec(memory_space=pltpu.VMEM)
    sds = jax.ShapeDtypeStruct
    ids = segment_ids.reshape(1, tokens)
    wide = 2 * SLOTS * HD + LANES

    def call(kernel, out_shape, in_specs, args, flops, moved, scratch=(), out_specs=None, limit=vmem_limit, **more):
        return pl.pallas_call(
            kernel,
            out_shape=out_shape,
            in_specs=in_specs,
            out_specs=jax.tree.map(lambda _: vmem, out_shape) if out_specs is None else out_specs,
            scratch_shapes=list(scratch),
            compiler_params=pltpu.CompilerParams(vmem_limit_bytes=limit),
            cost_estimate=pl.CostEstimate(flops=flops, bytes_accessed=moved, transcendentals=0),
            **more,
        )(*args)

    def shifted(block):
        return lax.ppermute(block, "seq", [(i - 1, i) for i in range(1, devices)])

    tail_steps = 2
    tail_key = call(
        functools.partial(tail_kernel, scale_rows), sds((half, width), bf16),
        [smem, pl.BlockSpec((half, width // tail_steps), lambda s: (1, s))], (block_scales, k_raw),
        half * width, 4 * half * width, grid=(tail_steps,), limit=whole_vmem,
        out_specs=pl.BlockSpec((half, width // tail_steps), lambda s: (0, s)),
    )
    prev_key = shifted(tail_key)
    table_steps = 4
    table_piece = width // table_steps
    table, tail_value = call(
        functools.partial(table_kernel, scale_rows),
        [sds((devices, heads, wide), bf16), sds((width, half), bf16)],
        [smem, pl.BlockSpec((1, tokens), lambda s: (0, 0))] + [pl.BlockSpec((tokens, table_piece), lambda s: (0, s))] * 2,
        (block_scales, ids, k_raw, v_raw),
        64 * tokens * width, 4 * tokens * width, grid=(table_steps,), limit=whole_vmem,
        out_specs=[pl.BlockSpec((devices, heads, wide), lambda s: (0, 0, 0)), pl.BlockSpec((table_piece, half), lambda s: (s, 0))],
        scratch=[pltpu.VMEM((heads, wide), f32), pltpu.VMEM((heads, 2, 8, HD), f32)],
    )
    table = lax.all_to_all(table, "seq", 0, 0, tiled=True)
    table = table.reshape(entries, wide)
    prev_value = shifted(tail_value)
    place = lax.axis_index("seq").astype(i32).reshape(1)
    gain = norm_gain.reshape(1, width)
    step_heads = 4
    steps = heads // step_heads
    piece = step_heads * HD

    def whole(*shape):
        return pl.BlockSpec(shape, lambda s: (0,) * len(shape))

    rows_in = pl.BlockSpec((tokens, piece), lambda s: (0, s))
    stat = pl.BlockSpec((1, step_heads, half), lambda s: (s, 0, 0))
    query, part, tops, totals, back, back_squares, prev_mask = call(
        functools.partial(main_kernel, scale_rows, devices),
        [sds((half, width), bf16), sds((width, half), f32), sds((steps, step_heads, half), f32),
         sds((steps, step_heads, half), f32), sds((half, width), f32), sds((1, half), f32), sds((half, half), f32)],
        [smem, smem, whole(1, tokens), whole(entries, wide), pl.BlockSpec((1, piece), lambda s: (0, s))] + [rows_in] * 3,
        (place, block_scales, ids, table, gain, q_raw, k_raw, v_raw),
        7 * half * tokens * width, 12 * tokens * width, grid=(steps,),
        out_specs=[
            pl.BlockSpec((half, piece), lambda s: (0, s)), pl.BlockSpec((piece, half), lambda s: (s, 0)), stat, stat,
            pl.BlockSpec((half, piece), lambda s: (0, s)), whole(1, half), whole(half, half),
        ],
        scratch=[
            pltpu.VMEM((half, half), f32), pltpu.VMEM((tokens, half), f32),
            pltpu.VMEM((SLOTS, land_pad, entries), bf16), pltpu.VMEM((land_pad, tokens), f32),
            pltpu.VMEM((land_pad, HD), f32),
        ],
    )
    front, squares = call(
        halo_kernel, [sds((half, width), f32), sds((1, tokens), f32)],
        [vmem] * 9, (query, part, tops, totals, gain, prev_mask, back_squares, prev_key, prev_value),
        2 * half * tokens * width, 8 * tokens * width,
    )
    parts = [squares] + [
        lax.ppermute(squares, "head", [(i, (i + d) % head_devices) for i in range(head_devices)])
        for d in range(1, head_devices)
    ]
    return call(
        functools.partial(scale_kernel, width * head_devices, head_devices), sds((tokens, width), bf16),
        [vmem] * (head_devices + 2), (*parts, front, back),
        3 * tokens * width, 6 * tokens * width, out_specs=pl.BlockSpec(memory_space=pl.ANY),
        scratch=[pltpu.VMEM((tokens, width), bf16), pltpu.SemaphoreType.DMA((tokens // LANES,))],
    )


def solution(mesh):
    in_specs = (
        P("seq", "head"), P("seq", "head"), P("seq", "head"),
        P(None, "seq", "head"), P("seq"), P("head"),
    )

    return jax.shard_map(on_device, mesh=mesh, in_specs=in_specs, out_specs=P("seq", "head"), check_vma=False)
```

```python
import functools
import math

import jax
import jax.numpy as jnp
from jax import lax
from jax.experimental import pallas as pl
from jax.experimental.pallas import tpu as pltpu
from jax.sharding import PartitionSpec as P


HD = 128
CAP = 4
LANES = 128
SLOTS = CAP + 2
EARLY = CAP + 1
epsilon = 1e-06
factor = math.log2(math.e) / math.sqrt(HD)
f32 = jnp.float32
bf16 = jnp.bfloat16
i32 = jnp.int32
vmem_limit = 20 * 2**20
whole_vmem = 60 * 1024 * 2**10
pipeline_depth = 2


def nt_dot(a, b):
    return lax.dot_general(a, b, (((1,), (1,)), ((), ())), preferred_element_type=f32)


def nn_dot(a, b):
    return jnp.dot(a, b, preferred_element_type=f32)


def iota(shape, axis):
    return lax.broadcasted_iota(i32, shape, axis)


def columns_of(row):
    pieces = []
    for start in range(0, row.shape[1], LANES):
        pieces.append(jnp.broadcast_to(row[:, start : start + LANES], (LANES, LANES)).T)
    return jnp.concatenate(pieces, axis=0)


def dequantized(raw, scales, which, head, cols, scale_rows, first=0):
    parts = []
    for piece in range(raw.shape[0] // scale_rows):
        rows = slice(piece * scale_rows, (piece + 1) * scale_rows)
        parts.append((raw[rows, cols].astype(f32) * scales[which, first + piece, head]).astype(bf16))
    return jnp.concatenate(parts, axis=0)


def table_kernel(scale_rows, pieces, scales, ids, k_raw, v_raw, table, tail_value, keys, values, sums, packed, tails, sems, out_sems):
    tokens = ids.shape[1]
    half = tokens // 2
    heads = sums.shape[0]
    piece = heads * HD // pieces
    copies = []
    for number in range(pieces):
        cols = slice(number * piece, (number + 1) * piece)
        for which, (source, target) in enumerate(((k_raw, keys), (v_raw, values))):
            copy = pltpu.make_async_copy(source.at[:, cols], target.at[:, cols], sems.at[number, which])
            copy.start()
            copies.append(copy)
    row = ids[...]
    local = row - row[:, 0:1]
    last = local[:, tokens - 1 :]
    slot = iota((2 * 8, tokens), 0)
    token = iota((2 * 8, tokens), 1)
    picked = (slot <= CAP) & (local == slot)
    picked = picked | ((slot == EARLY) & (local == last) & (token < half))
    picked = picked.astype(f32)
    pick = picked.astype(bf16)
    count = jnp.sum(picked, axis=1, keepdims=True).astype(i32)
    lane = iota((heads, LANES), 1)
    head_row = iota((heads, LANES), 0)
    meta = jnp.zeros((heads, LANES), i32)
    for index in range(SLOTS):
        seg = row[:, 0:1] + (last if index == EARLY else index)
        number = count[index : index + 1]
        for place, value in enumerate((seg & 127, seg >> 7, number & 127, number >> 7)):
            meta = jnp.where(lane == 4 * index + place, value, meta)
    tail_blocks = half // scale_rows
    scale = jnp.zeros((heads, LANES), f32)
    part = jnp.zeros((heads, LANES), i32)
    for block in range(tail_blocks):
        for head in range(heads):
            value = scales[1, scales.shape[1] - tail_blocks + block, head]
            here = (lane >= 4 * SLOTS + 3 * block) & (lane < 4 * SLOTS + 3 * block + 3)
            scale = jnp.where(here & (head_row == head), value, scale)
        for place in range(3):
            part = jnp.where(lane == 4 * SLOTS + 3 * block + place, place, part)
    high = scale.astype(bf16).astype(f32)
    middle = (scale - high).astype(bf16).astype(f32)
    low = scale - high - middle
    scale = jnp.where(part == 0, high, jnp.where(part == 1, middle, low))
    sums[:, 2 * SLOTS * HD :] = jnp.where(lane < 4 * SLOTS, meta.astype(f32), scale)
    writes = []
    for number in range(pieces):
        found = []
        for which, source in enumerate((keys, values)):
            copies[2 * number + which].wait()
            for head in range(number * piece // HD, (number + 1) * piece // HD):
                cols = slice(head * HD, (head + 1) * HD)
                value = dequantized(source, scales, 1 + which, head, cols, scale_rows)
                if which:
                    tails[:, cols] = value[half:]
                found.append((head, which * SLOTS, nn_dot(pick, value)))
        for head, start, total in found:
            for index in range(SLOTS):
                where = slice((start + index) * HD, (start + index + 1) * HD)
                sums[head : head + 1, where] = total[index : index + 1]
        cols = slice(number * piece, (number + 1) * piece)
        copy = pltpu.make_async_copy(tails.at[:, cols], tail_value.at[:, cols], out_sems.at[number])
        copy.start()
        writes.append(copy)
    packed[...] = jnp.broadcast_to(sums[...].astype(bf16)[None], packed.shape)
    copy = pltpu.make_async_copy(packed, table, out_sems.at[pieces])
    copy.start()
    writes.append(copy)
    for copy in writes:
        copy.wait()


def with_ones(value):
    return jnp.concatenate([value, jnp.ones((16, value.shape[1]), bf16)], axis=0)


def main_kernel(
    scale_rows, device_count,
    place, scales, ids, table, gain, q_raw, k_raw, v_raw, prev_raw,
    open_out, prev_weights, back_out, back_squares,
    near, far, picks, bias, inverse, prev_mask, prev_scales,
):
    step = pl.program_id(0)
    tokens = ids.shape[1]
    half = tokens // 2
    heads = q_raw.shape[1] // HD
    lands = CAP * device_count
    land_pad, entries = picks.shape[1:]
    all_heads = entries // device_count
    entry = iota((1, entries), 1)
    entry_device = entry // all_heads
    entry_head = entry - entry_device * all_heads

    @pl.when(step == 0)
    def _():
        me = place[0]
        row = ids[...]
        first = row[:, 0:1]
        column = columns_of(row)
        for mask, start, width in ((near, 0, half), (far, half, tokens)):
            for left in range(0, half, LANES):
                query = iota((width, LANES), 1) + (start + left)
                live = column[:width] == row[:, start + left : start + left + LANES]
                live = live & (iota((width, LANES), 0) <= query)
                mask[:, left : left + LANES] = jnp.where(live, 0.0, -jnp.inf)
        info = table[:, 2 * SLOTS * HD :].astype(f32).T
        land = iota((land_pad, entries), 0)
        count = jnp.zeros((land_pad, 1), f32)
        for index in range(SLOTS):
            seg = info[4 * index : 4 * index + 1] + 128.0 * info[4 * index + 1 : 4 * index + 2]
            number = info[4 * index + 2 : 4 * index + 3] + 128.0 * info[4 * index + 3 : 4 * index + 4]
            if index == EARLY:
                picked = (land == lands) & (entry_device == me - 1)
            else:
                is_open = seg == first.astype(f32)
                picked = (land < lands) & (land.astype(f32) == seg)
                picked = picked | ((land == lands) & is_open & (entry_device < me - 1))
                picked = picked | ((land == lands + 1) & is_open & (entry_device < me))
                picked = picked | ((land == lands + 2) & is_open & (entry_device == me - 1))
            picked = picked.astype(f32)
            picks[index] = picked.astype(bf16)
            count = count + jnp.sum(
                picked * jnp.where(entry_head == 0, number, 0.0), axis=1, keepdims=True
            )
        inverse[...] = jnp.broadcast_to(1.0 / jnp.maximum(count, 1.0), inverse.shape)
        amount = jnp.broadcast_to(count, (land_pad, LANES))
        log_count = jnp.log2(jnp.maximum(amount, 1.0))
        for left in range(0, tokens, LANES):
            seg = row[:, left : left + LANES]
            index = iota((land_pad, LANES), 0)
            run = lands if left < half else lands + 1
            live = ((index < lands) & (index < seg)) | ((index == run) & (seg == first) & (amount > 0.5))
            bias[:, left : left + LANES] = jnp.where(live, log_count, -jnp.inf)
        tail = count[lands + 2 : lands + 3].astype(i32)
        for left in range(0, half, LANES):
            live = (iota((half, LANES), 0) >= half - tail) & (row[:, left : left + LANES] == first)
            prev_mask[:, left : left + LANES] = jnp.where(live, 0.0, -jnp.inf)
        back_squares[...] = jnp.zeros(back_squares.shape, f32)
        info = table[:, 2 * SLOTS * HD :].astype(f32).reshape(device_count, all_heads, LANES)
        of_device = lax.broadcasted_iota(i32, info.shape, 0)
        info = jnp.sum(jnp.where(of_device == me - 1, info, 0.0), axis=0)
        for group in range(all_heads // heads):
            prev_scales[group] = info[group * heads : (group + 1) * heads]

    def prepared(head):
        cols = slice(head * HD, (head + 1) * HD)
        index = step * heads + head
        query = dequantized(q_raw, scales, 0, index, cols, scale_rows)
        key = dequantized(k_raw, scales, 1, index, cols, scale_rows)
        value = dequantized(v_raw, scales, 2, index, cols, scale_rows).T
        pieces = []
        for block in range(half // scale_rows):
            at = 4 * SLOTS + 3 * block
            parts = prev_scales[step, head : head + 1, at : at + 3]
            scale = parts[:, 0:1] + parts[:, 1:2] + parts[:, 2:3]
            raw = prev_raw[block * scale_rows : (block + 1) * scale_rows, cols]
            pieces.append((raw.astype(f32) * scale).astype(bf16))
        prev_key = jnp.concatenate(pieces, axis=0)
        mine = (entry_head == index).astype(f32).astype(bf16)
        land_key = jnp.zeros((land_pad, HD), f32)
        land_value = jnp.zeros((land_pad, HD), f32)
        for slot in range(SLOTS):
            pick = picks[slot] * mine
            land_key = land_key + nn_dot(pick, table[:, slot * HD : (slot + 1) * HD])
            land_value = land_value + nn_dot(pick, table[:, (SLOTS + slot) * HD : (SLOTS + slot + 1) * HD])
        land_key = (land_key * inverse[...]).astype(bf16)
        land_value = (land_value * inverse[...]).astype(bf16)
        land_value = jnp.concatenate([land_value, jnp.ones((land_pad, 16), bf16)], axis=1)
        return query, key, value, land_key, land_value, prev_key

    ready = {}

    def scores_of(task):
        head, part = task
        if head not in ready:
            ready[head] = prepared(head)
        query, key, _, land_key, _, prev_key = ready[head]
        rows = slice(part * half, (part + 1) * half)
        mask = far if part else near
        score = nt_dot(key[: (part + 1) * half], query[rows]) * factor + mask[...]
        land_score = nt_dot(land_key, query[rows]) * factor + bias[:, rows]
        if part:
            return score, land_score, None
        return score, land_score, nt_dot(prev_key, query[rows]) * factor + prev_mask[...]

    tasks = [(head, part) for head in range(heads) for part in range(2)]
    scores = [scores_of(task) for task in tasks[:pipeline_depth]]
    for number, (head, part) in enumerate(tasks):
        if number + pipeline_depth < len(tasks):
            scores.append(scores_of(tasks[number + pipeline_depth]))
        cols = slice(head * HD, (head + 1) * HD)
        score, land_score, prev_score = scores[number]
        _, _, value, _, land_value, _ = ready[head]
        top = jnp.maximum(
            jnp.max(score, axis=0, keepdims=True), jnp.max(land_score, axis=0, keepdims=True)
        )
        if part == 0:
            top = jnp.maximum(top, jnp.max(prev_score, axis=0, keepdims=True))
        weight = jnp.exp2(score - top).astype(bf16)
        land_weight = jnp.exp2(land_score - top).astype(bf16)
        found = nn_dot(with_ones(value[:, : (part + 1) * half]), weight)
        found = found + lax.dot_general(
            land_value, land_weight, (((0,), (0,)), ((), ())), preferred_element_type=f32
        )
        total = found[HD : HD + 1]
        if part == 0:
            prev_weight = jnp.exp2(prev_score - top)
            share = 1.0 / (total + jnp.sum(prev_weight, axis=0, keepdims=True))
            open_out[:, cols] = (found[:HD] * share).T
            prev_weights[head] = (prev_weight * share).astype(bf16).T
        else:
            done = found[:HD] * (1.0 / total)
            back_squares[...] += jnp.sum(done * done, axis=0, keepdims=True)
            back_out[:, cols] = done.T * gain[:, cols]


def halo_kernel(opened, prev_weights, gain, back_squares, prev_value, out, squares):
    heads, half = prev_weights.shape[:2]
    found = []
    power = jnp.zeros((half, HD), f32)
    for head in range(heads + pipeline_depth):
        if head < heads:
            found.append(nn_dot(prev_weights[head], prev_value[:, head * HD : (head + 1) * HD]))
        done = head - pipeline_depth
        if done >= 0:
            cols = slice(done * HD, (done + 1) * HD)
            value = opened[:, cols] + found[done]
            power = power + value * value
            out[:, cols] = value * gain[:, cols]
    for start in range(0, half, LANES):
        total = jnp.sum(power[start : start + LANES].T, axis=0, keepdims=True)
        squares[:, start : start + LANES] = total
    squares[:, half:] = back_squares[...]


def scale_kernel(width, count, *refs):
    parts, (front, back, out, ready, sems) = refs[:count], refs[count:]
    total = parts[0][...]
    for ref in parts[1:]:
        total = total + ref[...]
    norm = columns_of(lax.rsqrt(total / width + epsilon))
    half = front.shape[0]
    copies = []
    for part, source in enumerate((front, back)):
        for start in range(0, half, LANES):
            rows = slice(part * half + start, part * half + start + LANES)
            for left in range(0, front.shape[1], LANES):
                cols = slice(left, left + LANES)
                ready[rows, cols] = (source[start : start + LANES, cols] * norm[rows]).astype(bf16)
            copy = pltpu.make_async_copy(ready.at[rows], out.at[rows], sems.at[len(copies)])
            copy.start()
            copies.append(copy)
    for copy in copies:
        copy.wait()


def on_device(q_raw, k_raw, v_raw, block_scales, segment_ids, norm_gain):
    tokens, width = q_raw.shape
    half = tokens // 2
    heads = width // HD
    scale_rows = tokens // block_scales.shape[1]
    devices = lax.axis_size("seq")
    head_devices = lax.axis_size("head")
    entries = devices * heads
    land_pad = -(-(CAP * devices + 3) // 16) * 16
    smem = pl.BlockSpec(memory_space=pltpu.SMEM)
    vmem = pl.BlockSpec(memory_space=pltpu.VMEM)
    hbm = pl.BlockSpec(memory_space=pltpu.HBM)
    sds = jax.ShapeDtypeStruct
    ids = segment_ids.reshape(1, tokens)
    wide = 2 * SLOTS * HD + LANES

    def call(kernel, out_shape, in_specs, args, flops, moved, scratch=(), out_specs=None, limit=vmem_limit, **more):
        return pl.pallas_call(
            kernel,
            out_shape=out_shape,
            in_specs=in_specs,
            out_specs=jax.tree.map(lambda _: vmem, out_shape) if out_specs is None else out_specs,
            scratch_shapes=list(scratch),
            compiler_params=pltpu.CompilerParams(vmem_limit_bytes=limit),
            cost_estimate=pl.CostEstimate(flops=flops, bytes_accessed=moved, transcendentals=0),
            **more,
        )(*args)

    def shifted(block):
        return lax.ppermute(block, "seq", [(i - 1, i) for i in range(1, devices)])

    prev_key = shifted(k_raw[half:])
    table_pieces = 4
    table, tail_value = call(
        functools.partial(table_kernel, scale_rows, table_pieces),
        [sds((devices, heads, wide), bf16), sds((half, width), bf16)],
        [smem, vmem, hbm, hbm], (block_scales, ids, k_raw, v_raw),
        64 * tokens * width, 4 * tokens * width, out_specs=[hbm, hbm], limit=whole_vmem,
        scratch=[
            pltpu.VMEM((tokens, width), bf16), pltpu.VMEM((tokens, width), bf16),
            pltpu.VMEM((heads, wide), f32), pltpu.VMEM((devices, heads, wide), bf16), pltpu.VMEM((half, width), bf16),
            pltpu.SemaphoreType.DMA((table_pieces, 2)), pltpu.SemaphoreType.DMA((table_pieces + 1,)),
        ],
    )
    table = lax.all_to_all(table, "seq", 0, 0, tiled=True)
    table = table.reshape(entries, wide)
    prev_value = shifted(tail_value)
    place = lax.axis_index("seq").astype(i32).reshape(1)
    gain = norm_gain.reshape(1, width)
    step_heads = 4
    steps = heads // step_heads
    piece = step_heads * HD

    def whole(*shape):
        return pl.BlockSpec(shape, lambda s: (0,) * len(shape))

    rows_in = pl.BlockSpec((tokens, piece), lambda s: (0, s))
    half_rows = pl.BlockSpec((half, piece), lambda s: (0, s))
    opened, prev_weights, back, back_squares = call(
        functools.partial(main_kernel, scale_rows, devices),
        [sds((half, width), f32), sds((heads, half, half), bf16), sds((half, width), f32), sds((1, half), f32)],
        [smem, smem, whole(1, tokens), whole(entries, wide), pl.BlockSpec((1, piece), lambda s: (0, s))] + [rows_in] * 3 + [half_rows],
        (place, block_scales, ids, table, gain, *(pltpu.with_memory_space_constraint(x, pltpu.HBM) for x in (q_raw, k_raw, v_raw)), prev_key),
        8 * half * tokens * width, 12 * tokens * width, grid=(steps,),
        out_specs=[half_rows, pl.BlockSpec((step_heads, half, half), lambda s: (s, 0, 0)), half_rows, whole(1, half)],
        scratch=[
            pltpu.VMEM((half, half), f32), pltpu.VMEM((tokens, half), f32),
            pltpu.VMEM((SLOTS, land_pad, entries), bf16), pltpu.VMEM((land_pad, tokens), f32),
            pltpu.VMEM((land_pad, HD), f32), pltpu.VMEM((half, half), f32), pltpu.VMEM((steps, step_heads, LANES), f32),
        ],
    )
    front, squares = call(
        halo_kernel, [sds((half, width), f32), sds((1, tokens), f32)],
        [vmem] * 5, (opened, prev_weights, gain, back_squares, prev_value),
        half * half * width * 2, 8 * tokens * width,
    )
    pairs = head_devices & (head_devices - 1) == 0
    parts = [squares] + [
        lax.ppermute(squares, "head", [(i, i ^ d if pairs else (i + d) % head_devices) for i in range(head_devices)])
        for d in range(1, head_devices)
    ]
    return call(
        functools.partial(scale_kernel, width * head_devices, head_devices), sds((tokens, width), bf16),
        [vmem] * (head_devices + 2), (*parts, front, back),
        3 * tokens * width, 6 * tokens * width, out_specs=pl.BlockSpec(memory_space=pl.ANY),
        scratch=[pltpu.VMEM((tokens, width), bf16), pltpu.SemaphoreType.DMA((tokens // LANES,))],
    )


def solution(mesh):
    in_specs = (
        P("seq", "head"), P("seq", "head"), P("seq", "head"),
        P(None, "seq", "head"), P("seq"), P("head"),
    )

    return jax.shard_map(on_device, mesh=mesh, in_specs=in_specs, out_specs=P("seq", "head"), check_vma=False)
```

```python
import functools
import math

import jax
import jax.numpy as jnp
from jax import lax
from jax.experimental import pallas as pl
from jax.experimental.pallas import tpu as pltpu
from jax.sharding import PartitionSpec as P


HD = 128
CAP = 4
LANES = 128
SLOTS = CAP + 2
EARLY = CAP + 1
epsilon = 1e-06
factor = math.log2(math.e) / math.sqrt(HD)
f32 = jnp.float32
bf16 = jnp.bfloat16
i32 = jnp.int32
vmem_limit = 20 * 2**20
whole_vmem = 60 * 1024 * 2**10
pipeline_depth = 2


def nt_dot(a, b):
    return lax.dot_general(a, b, (((1,), (1,)), ((), ())), preferred_element_type=f32)


def nn_dot(a, b):
    return jnp.dot(a, b, preferred_element_type=f32)


def iota(shape, axis):
    return lax.broadcasted_iota(i32, shape, axis)


def columns_of(row):
    pieces = []
    for start in range(0, row.shape[1], LANES):
        pieces.append(jnp.broadcast_to(row[:, start : start + LANES], (LANES, LANES)).T)
    return jnp.concatenate(pieces, axis=0)


def dequantized(raw, scales, which, head, cols, scale_rows, first=0):
    parts = []
    for piece in range(raw.shape[0] // scale_rows):
        rows = slice(piece * scale_rows, (piece + 1) * scale_rows)
        parts.append((raw[rows, cols].astype(f32) * scales[which, first + piece, head]).astype(bf16))
    return jnp.concatenate(parts, axis=0)


def table_kernel(scale_rows, pieces, scales, ids, k_raw, v_raw, table, tail_value, keys, values, sums, packed, tails, sems, out_sems):
    tokens = ids.shape[1]
    half = tokens // 2
    heads = sums.shape[0]
    piece = heads * HD // pieces
    copies = []
    for number in range(pieces):
        cols = slice(number * piece, (number + 1) * piece)
        for which, (source, target) in enumerate(((k_raw, keys), (v_raw, values))):
            copy = pltpu.make_async_copy(source.at[:, cols], target.at[:, cols], sems.at[number, which])
            copy.start()
            copies.append(copy)
    row = ids[...]
    local = row - row[:, 0:1]
    last = local[:, tokens - 1 :]
    slot = iota((2 * 8, tokens), 0)
    token = iota((2 * 8, tokens), 1)
    picked = (slot <= CAP) & (local == slot)
    picked = picked | ((slot == EARLY) & (local == last) & (token < half))
    picked = picked.astype(f32)
    pick = picked.astype(bf16)
    count = jnp.sum(picked, axis=1, keepdims=True).astype(i32)
    lane = iota((heads, LANES), 1)
    head_row = iota((heads, LANES), 0)
    meta = jnp.zeros((heads, LANES), i32)
    for index in range(SLOTS):
        seg = row[:, 0:1] + (last if index == EARLY else index)
        number = count[index : index + 1]
        for place, value in enumerate((seg & 127, seg >> 7, number & 127, number >> 7)):
            meta = jnp.where(lane == 4 * index + place, value, meta)
    tail_blocks = half // scale_rows
    scale = jnp.zeros((heads, LANES), f32)
    part = jnp.zeros((heads, LANES), i32)
    for block in range(tail_blocks):
        for head in range(heads):
            value = scales[1, scales.shape[1] - tail_blocks + block, head]
            here = (lane >= 4 * SLOTS + 3 * block) & (lane < 4 * SLOTS + 3 * block + 3)
            scale = jnp.where(here & (head_row == head), value, scale)
        for place in range(3):
            part = jnp.where(lane == 4 * SLOTS + 3 * block + place, place, part)
    high = scale.astype(bf16).astype(f32)
    middle = (scale - high).astype(bf16).astype(f32)
    low = scale - high - middle
    scale = jnp.where(part == 0, high, jnp.where(part == 1, middle, low))
    sums[:, 2 * SLOTS * HD :] = jnp.where(lane < 4 * SLOTS, meta.astype(f32), scale)
    writes = []
    for number in range(pieces):
        found = []
        for which, source in enumerate((keys, values)):
            copies[2 * number + which].wait()
            for head in range(number * piece // HD, (number + 1) * piece // HD):
                cols = slice(head * HD, (head + 1) * HD)
                value = dequantized(source, scales, 1 + which, head, cols, scale_rows)
                if which:
                    tails[:, cols] = value[half:]
                found.append((head, which * SLOTS, nn_dot(pick, value)))
        for head, start, total in found:
            for index in range(SLOTS):
                where = slice((start + index) * HD, (start + index + 1) * HD)
                sums[head : head + 1, where] = total[index : index + 1]
        cols = slice(number * piece, (number + 1) * piece)
        copy = pltpu.make_async_copy(tails.at[:, cols], tail_value.at[:, cols], out_sems.at[number])
        copy.start()
        writes.append(copy)
    packed[...] = jnp.broadcast_to(sums[...].astype(bf16)[None], packed.shape)
    copy = pltpu.make_async_copy(packed, table, out_sems.at[pieces])
    copy.start()
    writes.append(copy)
    for copy in writes:
        copy.wait()


def with_ones(value):
    return jnp.concatenate([value, jnp.ones((16, value.shape[1]), bf16)], axis=0)


def main_kernel(
    scale_rows, device_count,
    place, scales, ids, table, gain, q_raw, k_raw, v_raw, prev_raw,
    open_out, prev_weights, back_out, back_squares,
    near, far, picks, bias, inverse, prev_mask, prev_scales,
):
    step = pl.program_id(0)
    tokens = ids.shape[1]
    half = tokens // 2
    heads = q_raw.shape[1] // HD
    lands = CAP * device_count
    land_pad, entries = picks.shape[1:]
    all_heads = entries // device_count
    entry = iota((1, entries), 1)
    entry_device = entry // all_heads
    entry_head = entry - entry_device * all_heads

    @pl.when(step == 0)
    def _():
        me = place[0]
        row = ids[...]
        first = row[:, 0:1]
        column = columns_of(row)
        for mask, start, width in ((near, 0, half), (far, half, tokens)):
            for left in range(0, half, LANES):
                query = iota((width, LANES), 1) + (start + left)
                live = column[:width] == row[:, start + left : start + left + LANES]
                live = live & (iota((width, LANES), 0) <= query)
                mask[:, left : left + LANES] = jnp.where(live, 0.0, -jnp.inf)
        info = table[:, 2 * SLOTS * HD :].astype(f32).T
        land = iota((land_pad, entries), 0)
        count = jnp.zeros((land_pad, 1), f32)
        for index in range(SLOTS):
            seg = info[4 * index : 4 * index + 1] + 128.0 * info[4 * index + 1 : 4 * index + 2]
            number = info[4 * index + 2 : 4 * index + 3] + 128.0 * info[4 * index + 3 : 4 * index + 4]
            if index == EARLY:
                picked = (land == lands) & (entry_device == me - 1)
            else:
                is_open = seg == first.astype(f32)
                picked = (land < lands) & (land.astype(f32) == seg)
                picked = picked | ((land == lands) & is_open & (entry_device < me - 1))
                picked = picked | ((land == lands + 1) & is_open & (entry_device < me))
                picked = picked | ((land == lands + 2) & is_open & (entry_device == me - 1))
            picked = picked.astype(f32)
            picks[index] = picked.astype(bf16)
            count = count + jnp.sum(
                picked * jnp.where(entry_head == 0, number, 0.0), axis=1, keepdims=True
            )
        inverse[...] = jnp.broadcast_to(1.0 / jnp.maximum(count, 1.0), inverse.shape)
        amount = jnp.broadcast_to(count, (land_pad, LANES))
        log_count = jnp.log2(jnp.maximum(amount, 1.0))
        for left in range(0, tokens, LANES):
            seg = row[:, left : left + LANES]
            index = iota((land_pad, LANES), 0)
            run = lands if left < half else lands + 1
            live = ((index < lands) & (index < seg)) | ((index == run) & (seg == first) & (amount > 0.5))
            bias[:, left : left + LANES] = jnp.where(live, log_count, -jnp.inf)
        tail = count[lands + 2 : lands + 3].astype(i32)
        for left in range(0, half, LANES):
            live = (iota((half, LANES), 0) >= half - tail) & (row[:, left : left + LANES] == first)
            prev_mask[:, left : left + LANES] = jnp.where(live, 0.0, -jnp.inf)
        back_squares[...] = jnp.zeros(back_squares.shape, f32)
        info = table[:, 2 * SLOTS * HD :].astype(f32).reshape(device_count, all_heads, LANES)
        of_device = lax.broadcasted_iota(i32, info.shape, 0)
        info = jnp.sum(jnp.where(of_device == me - 1, info, 0.0), axis=0)
        for group in range(all_heads // heads):
            prev_scales[group] = info[group * heads : (group + 1) * heads]

    def prepared(head):
        cols = slice(head * HD, (head + 1) * HD)
        index = step * heads + head
        query = dequantized(q_raw, scales, 0, index, cols, scale_rows)
        key = dequantized(k_raw, scales, 1, index, cols, scale_rows)
        value = dequantized(v_raw, scales, 2, index, cols, scale_rows).T
        pieces = []
        for block in range(half // scale_rows):
            at = 4 * SLOTS + 3 * block
            parts = prev_scales[step, head : head + 1, at : at + 3]
            scale = parts[:, 0:1] + parts[:, 1:2] + parts[:, 2:3]
            raw = prev_raw[block * scale_rows : (block + 1) * scale_rows, cols]
            pieces.append((raw.astype(f32) * scale).astype(bf16))
        prev_key = jnp.concatenate(pieces, axis=0)
        mine = (entry_head == index).astype(f32).astype(bf16)
        land_key = jnp.zeros((land_pad, HD), f32)
        land_value = jnp.zeros((land_pad, HD), f32)
        for slot in range(SLOTS):
            pick = picks[slot] * mine
            land_key = land_key + nn_dot(pick, table[:, slot * HD : (slot + 1) * HD])
            land_value = land_value + nn_dot(pick, table[:, (SLOTS + slot) * HD : (SLOTS + slot + 1) * HD])
        land_key = (land_key * inverse[...]).astype(bf16)
        land_value = (land_value * inverse[...]).astype(bf16)
        land_value = jnp.concatenate([land_value, jnp.ones((land_pad, 16), bf16)], axis=1)
        return query, key, value, land_key, land_value, prev_key

    ready = {}

    def scores_of(task):
        head, part = task
        if head not in ready:
            ready[head] = prepared(head)
        query, key, _, land_key, _, prev_key = ready[head]
        rows = slice(part * half, (part + 1) * half)
        mask = far if part else near
        score = nt_dot(key[: (part + 1) * half], query[rows]) * factor + mask[...]
        land_score = nt_dot(land_key, query[rows]) * factor + bias[:, rows]
        if part:
            return score, land_score, None
        return score, land_score, nt_dot(prev_key, query[rows]) * factor + prev_mask[...]

    tasks = [(head, part) for head in range(heads) for part in range(2)]
    scores = [scores_of(task) for task in tasks[:pipeline_depth]]
    for number, (head, part) in enumerate(tasks):
        if number + pipeline_depth < len(tasks):
            scores.append(scores_of(tasks[number + pipeline_depth]))
        cols = slice(head * HD, (head + 1) * HD)
        score, land_score, prev_score = scores[number]
        _, _, value, _, land_value, _ = ready[head]
        top = jnp.maximum(
            jnp.max(score, axis=0, keepdims=True), jnp.max(land_score, axis=0, keepdims=True)
        )
        if part == 0:
            top = jnp.maximum(top, jnp.max(prev_score, axis=0, keepdims=True))
        weight = jnp.exp2(score - top).astype(bf16)
        land_weight = jnp.exp2(land_score - top).astype(bf16)
        found = nn_dot(with_ones(value[:, : (part + 1) * half]), weight)
        found = found + lax.dot_general(
            land_value, land_weight, (((0,), (0,)), ((), ())), preferred_element_type=f32
        )
        total = found[HD : HD + 1]
        if part == 0:
            prev_weight = jnp.exp2(prev_score - top)
            share = 1.0 / (total + jnp.sum(prev_weight, axis=0, keepdims=True))
            open_out[:, cols] = (found[:HD] * share).T
            prev_weights[head] = (prev_weight * share).astype(bf16).T
        else:
            done = found[:HD] * (1.0 / total)
            back_squares[...] += jnp.sum(done * done, axis=0, keepdims=True)
            back_out[:, cols] = done.T * gain[:, cols]


def halo_kernel(opened, prev_weights, gain, back_squares, prev_value, out, squares):
    heads, half = prev_weights.shape[:2]
    found = []
    power = jnp.zeros((half, HD), f32)
    for head in range(heads + pipeline_depth):
        if head < heads:
            found.append(nn_dot(prev_weights[head], prev_value[:, head * HD : (head + 1) * HD]))
        done = head - pipeline_depth
        if done >= 0:
            cols = slice(done * HD, (done + 1) * HD)
            value = opened[:, cols] + found[done]
            power = power + value * value
            out[:, cols] = value * gain[:, cols]
    for start in range(0, half, LANES):
        total = jnp.sum(power[start : start + LANES].T, axis=0, keepdims=True)
        squares[:, start : start + LANES] = total
    squares[:, half:] = back_squares[...]


def scale_kernel(width, count, *refs):
    parts, (front, back, out, ready, sems) = refs[:count], refs[count:]
    total = parts[0][...]
    for ref in parts[1:]:
        total = total + ref[...]
    norm = columns_of(lax.rsqrt(total / width + epsilon))
    half = front.shape[0]
    copies = []
    for part, source in enumerate((front, back)):
        for start in range(0, half, LANES):
            rows = slice(part * half + start, part * half + start + LANES)
            for left in range(0, front.shape[1], LANES):
                cols = slice(left, left + LANES)
                ready[rows, cols] = (source[start : start + LANES, cols] * norm[rows]).astype(bf16)
            copy = pltpu.make_async_copy(ready.at[rows], out.at[rows], sems.at[len(copies)])
            copy.start()
            copies.append(copy)
    for copy in copies:
        copy.wait()


def on_device(q_raw, k_raw, v_raw, block_scales, segment_ids, norm_gain):
    tokens, width = q_raw.shape
    half = tokens // 2
    heads = width // HD
    scale_rows = tokens // block_scales.shape[1]
    devices = lax.axis_size("seq")
    head_devices = lax.axis_size("head")
    entries = devices * heads
    land_pad = -(-(CAP * devices + 3) // 16) * 16
    smem = pl.BlockSpec(memory_space=pltpu.SMEM)
    vmem = pl.BlockSpec(memory_space=pltpu.VMEM)
    hbm = pl.BlockSpec(memory_space=pltpu.HBM)
    sds = jax.ShapeDtypeStruct
    ids = segment_ids.reshape(1, tokens)
    wide = 2 * SLOTS * HD + LANES

    def call(kernel, out_shape, in_specs, args, flops, moved, scratch=(), out_specs=None, limit=vmem_limit, **more):
        return pl.pallas_call(
            kernel,
            out_shape=out_shape,
            in_specs=in_specs,
            out_specs=jax.tree.map(lambda _: vmem, out_shape) if out_specs is None else out_specs,
            scratch_shapes=list(scratch),
            compiler_params=pltpu.CompilerParams(vmem_limit_bytes=limit),
            cost_estimate=pl.CostEstimate(flops=flops, bytes_accessed=moved, transcendentals=0),
            **more,
        )(*args)

    prev_key = lax.ppermute(k_raw[half:], "seq", [(i, (i + 1) % devices) for i in range(devices)])
    table_pieces = 4
    table, tail_value = call(
        functools.partial(table_kernel, scale_rows, table_pieces),
        [sds((devices, heads, wide), bf16), sds((half, width), bf16)],
        [smem, vmem, hbm, hbm], (block_scales, ids, k_raw, v_raw),
        64 * tokens * width, 4 * tokens * width, out_specs=[hbm, hbm], limit=whole_vmem,
        scratch=[
            pltpu.VMEM((tokens, width), bf16), pltpu.VMEM((tokens, width), bf16),
            pltpu.VMEM((heads, wide), f32), pltpu.VMEM((devices, heads, wide), bf16), pltpu.VMEM((half, width), bf16),
            pltpu.SemaphoreType.DMA((table_pieces, 2)), pltpu.SemaphoreType.DMA((table_pieces + 1,)),
        ],
    )
    table = lax.all_to_all(table, "seq", 0, 0, tiled=True)
    table = table.reshape(entries, wide)
    prev_value = lax.ppermute(tail_value, "seq", [(i - 1, i) for i in range(1, devices)])
    place = lax.axis_index("seq").astype(i32).reshape(1)
    gain = norm_gain.reshape(1, width)
    step_heads = 4
    steps = heads // step_heads
    piece = step_heads * HD

    def whole(*shape):
        return pl.BlockSpec(shape, lambda s: (0,) * len(shape))

    rows_in = pl.BlockSpec((tokens, piece), lambda s: (0, s))
    half_rows = pl.BlockSpec((half, piece), lambda s: (0, s))
    opened, prev_weights, back, back_squares = call(
        functools.partial(main_kernel, scale_rows, devices),
        [sds((half, width), f32), sds((heads, half, half), bf16), sds((half, width), f32), sds((1, half), f32)],
        [smem, smem, whole(1, tokens), whole(entries, wide), pl.BlockSpec((1, piece), lambda s: (0, s))] + [rows_in] * 3 + [half_rows],
        (place, block_scales, ids, table, gain, *(pltpu.with_memory_space_constraint(x, pltpu.HBM) for x in (q_raw, k_raw, v_raw)), prev_key),
        8 * half * tokens * width, 12 * tokens * width, grid=(steps,),
        out_specs=[half_rows, pl.BlockSpec((step_heads, half, half), lambda s: (s, 0, 0)), half_rows, whole(1, half)],
        scratch=[
            pltpu.VMEM((half, half), f32), pltpu.VMEM((tokens, half), f32),
            pltpu.VMEM((SLOTS, land_pad, entries), bf16), pltpu.VMEM((land_pad, tokens), f32),
            pltpu.VMEM((land_pad, HD), f32), pltpu.VMEM((half, half), f32), pltpu.VMEM((steps, step_heads, LANES), f32),
        ],
    )
    front, squares = call(
        halo_kernel, [sds((half, width), f32), sds((1, tokens), f32)],
        [vmem] * 5, (opened, prev_weights, gain, back_squares, prev_value),
        half * half * width * 2, 8 * tokens * width,
    )
    pairs = head_devices & (head_devices - 1) == 0
    parts = [squares] + [
        lax.ppermute(squares, "head", [(i, i ^ d if pairs else (i + d) % head_devices) for i in range(head_devices)])
        for d in range(1, head_devices)
    ]
    return call(
        functools.partial(scale_kernel, width * head_devices, head_devices), sds((tokens, width), bf16),
        [vmem] * (head_devices + 2), (*parts, front, back),
        3 * tokens * width, 6 * tokens * width, out_specs=pl.BlockSpec(memory_space=pl.ANY),
        scratch=[pltpu.VMEM((tokens, width), bf16), pltpu.SemaphoreType.DMA((tokens // LANES,))],
    )


def solution(mesh):
    in_specs = (
        P("seq", "head"), P("seq", "head"), P("seq", "head"),
        P(None, "seq", "head"), P("seq"), P("head"),
    )

    return jax.shard_map(on_device, mesh=mesh, in_specs=in_specs, out_specs=P("seq", "head"), check_vma=False)
```

```python
import functools
import math

import jax
import jax.numpy as jnp
from jax import lax
from jax.experimental import pallas as pl
from jax.experimental.pallas import tpu as pltpu
from jax.sharding import PartitionSpec as P


HD = 128
CAP = 4
LANES = 128
SLOTS = CAP + 1
EARLY = CAP + 1
epsilon = 1e-06
factor = math.log2(math.e) / math.sqrt(HD)
f32 = jnp.float32
bf16 = jnp.bfloat16
i32 = jnp.int32
vmem_limit = 20 * 2**20
whole_vmem = 60 * 1024 * 2**10
pipeline_depth = 2


def nt_dot(a, b):
    return lax.dot_general(a, b, (((1,), (1,)), ((), ())), preferred_element_type=f32)


def nn_dot(a, b):
    return jnp.dot(a, b, preferred_element_type=f32)


def iota(shape, axis):
    return lax.broadcasted_iota(i32, shape, axis)


def columns_of(row):
    pieces = []
    for start in range(0, row.shape[1], LANES):
        pieces.append(jnp.broadcast_to(row[:, start : start + LANES], (LANES, LANES)).T)
    return jnp.concatenate(pieces, axis=0)


def dequantized(raw, scales, which, head, cols, scale_rows, first=0):
    parts = []
    for piece in range(raw.shape[0] // scale_rows):
        rows = slice(piece * scale_rows, (piece + 1) * scale_rows)
        parts.append((raw[rows, cols].astype(f32) * scales[which, first + piece, head]).astype(bf16))
    return jnp.concatenate(parts, axis=0)


def table_kernel(
    scale_rows, pieces, scales_in, ids_in, k_raw, v_raw, table, tail_value, extra_out,
    scales, ids, keys, values, sums, packed, tails, extra, extra_packed, sems, small_sems, out_sems,
):
    tokens = ids.shape[1]
    half = tokens // 2
    heads = sums.shape[0]
    piece = heads * HD // pieces
    small = [
        pltpu.make_async_copy(scales_in, scales, small_sems.at[0]),
        pltpu.make_async_copy(ids_in, ids, small_sems.at[1]),
    ]
    for copy in small:
        copy.start()
    copies = []
    for number in range(pieces):
        cols = slice(number * piece, (number + 1) * piece)
        for which, (source, target) in enumerate(((k_raw, keys), (v_raw, values))):
            copy = pltpu.make_async_copy(source.at[:, cols], target.at[:, cols], sems.at[number, which])
            copy.start()
            copies.append(copy)
    for copy in small:
        copy.wait()
    row = ids[...]
    local = row - row[:, 0:1]
    last = local[:, tokens - 1 :]
    slot = iota((2 * 8, tokens), 0)
    token = iota((2 * 8, tokens), 1)
    picked = (slot <= CAP) & (local == slot)
    picked = picked | ((slot == EARLY) & (local == last) & (token < half))
    picked = picked.astype(f32)
    pick = picked.astype(bf16)
    count = jnp.sum(picked, axis=1, keepdims=True).astype(i32)
    lane = iota((heads, LANES), 1)
    head_row = iota((heads, LANES), 0)
    meta = jnp.zeros((heads, LANES), i32)
    for index in range(SLOTS):
        seg = row[:, 0:1] + index
        number = count[index : index + 1]
        for place, value in enumerate((seg & 127, seg >> 7, number & 127, number >> 7)):
            meta = jnp.where(lane == 4 * index + place, value, meta)
    sums[:, 2 * SLOTS * HD :] = meta.astype(f32)
    number = count[EARLY : EARLY + 1]
    meta = jnp.where(lane == 0, number & 127, jnp.where(lane == 1, number >> 7, 0))
    tail_blocks = half // scale_rows
    scale = jnp.zeros((heads, LANES), f32)
    part = jnp.zeros((heads, LANES), i32)
    for block in range(tail_blocks):
        for head in range(heads):
            value = scales[1, scales.shape[1] - tail_blocks + block, head]
            here = (lane >= 2 + 3 * block) & (lane < 5 + 3 * block)
            scale = jnp.where(here & (head_row == head), value, scale)
        for place in range(3):
            part = jnp.where(lane == 2 + 3 * block + place, place, part)
    high = scale.astype(bf16).astype(f32)
    middle = (scale - high).astype(bf16).astype(f32)
    low = scale - high - middle
    scale = jnp.where(part == 0, high, jnp.where(part == 1, middle, low))
    extra[:, 2 * HD :] = jnp.where(lane < 2, meta.astype(f32), scale)
    writes = []
    for number in range(pieces):
        found = []
        for which, source in enumerate((keys, values)):
            copies[2 * number + which].wait()
            for head in range(number * piece // HD, (number + 1) * piece // HD):
                cols = slice(head * HD, (head + 1) * HD)
                value = dequantized(source, scales, 1 + which, head, cols, scale_rows)
                if which:
                    tails[:, cols] = value[half:]
                found.append((head, which, nn_dot(pick, value)))
        for head, which, total in found:
            for index in range(SLOTS):
                where = slice((which * SLOTS + index) * HD, (which * SLOTS + index + 1) * HD)
                sums[head : head + 1, where] = total[index : index + 1]
            extra[head : head + 1, which * HD : (which + 1) * HD] = total[EARLY : EARLY + 1]
        cols = slice(number * piece, (number + 1) * piece)
        copy = pltpu.make_async_copy(tails.at[:, cols], tail_value.at[:, cols], out_sems.at[number])
        copy.start()
        writes.append(copy)
    packed[...] = jnp.broadcast_to(sums[...].astype(bf16)[None], packed.shape)
    extra_packed[...] = extra[...].astype(bf16)
    for number, (source, target) in enumerate(((packed, table), (extra_packed, extra_out))):
        copy = pltpu.make_async_copy(source, target, out_sems.at[pieces + number])
        copy.start()
        writes.append(copy)
    for copy in writes:
        copy.wait()


def with_ones(value):
    return jnp.concatenate([value, jnp.ones((16, value.shape[1]), bf16)], axis=0)


def main_kernel(
    scale_rows, device_count,
    place, scales, ids, table, extra, gain, q_raw, k_raw, v_raw, prev_raw,
    open_out, prev_weights, back_out, back_squares,
    near, far, picks, bias, inverse, prev_mask, extras, is_early,
):
    step = pl.program_id(0)
    tokens = ids.shape[1]
    half = tokens // 2
    heads = q_raw.shape[1] // HD
    lands = CAP * device_count
    land_pad, entries = picks.shape[1:]
    all_heads = entries // device_count
    entry = iota((1, entries), 1)
    entry_device = entry // all_heads
    entry_head = entry - entry_device * all_heads

    @pl.when(step == 0)
    def _():
        me = place[0]
        row = ids[...]
        first = row[:, 0:1]
        column = columns_of(row)
        for mask, start, width in ((near, 0, half), (far, half, tokens)):
            for left in range(0, half, LANES):
                query = iota((width, LANES), 1) + (start + left)
                live = column[:width] == row[:, start + left : start + left + LANES]
                live = live & (iota((width, LANES), 0) <= query)
                mask[:, left : left + LANES] = jnp.where(live, 0.0, -jnp.inf)
        info = table[:, 2 * SLOTS * HD :].astype(f32).T
        land = iota((land_pad, entries), 0)
        count = jnp.zeros((land_pad, 1), f32)
        for index in range(SLOTS):
            seg = info[4 * index : 4 * index + 1] + 128.0 * info[4 * index + 1 : 4 * index + 2]
            number = info[4 * index + 2 : 4 * index + 3] + 128.0 * info[4 * index + 3 : 4 * index + 4]
            is_open = seg == first.astype(f32)
            picked = (land < lands) & (land.astype(f32) == seg)
            picked = picked | ((land == lands) & is_open & (entry_device < me - 1))
            picked = picked | ((land == lands + 1) & is_open & (entry_device < me))
            picked = picked | ((land == lands + 2) & is_open & (entry_device == me - 1))
            picked = picked.astype(f32)
            picks[index] = picked.astype(bf16)
            count = count + jnp.sum(
                picked * jnp.where(entry_head == 0, number, 0.0), axis=1, keepdims=True
            )
        early = ((iota((land_pad, HD), 0) == lands) & (me > 0)).astype(f32)
        is_early[...] = early
        info = extra[...].astype(f32)
        for group in range(all_heads // heads):
            extras[group] = info[group * heads : (group + 1) * heads]
        count = count + early[:, 0:1] * (info[0:1, 2 * HD : 2 * HD + 1] + 128.0 * info[0:1, 2 * HD + 1 : 2 * HD + 2])
        inverse[...] = jnp.broadcast_to(1.0 / jnp.maximum(count, 1.0), inverse.shape)
        amount = jnp.broadcast_to(count, (land_pad, LANES))
        log_count = jnp.log2(jnp.maximum(amount, 1.0))
        for left in range(0, tokens, LANES):
            seg = row[:, left : left + LANES]
            index = iota((land_pad, LANES), 0)
            run = lands if left < half else lands + 1
            live = ((index < lands) & (index < seg)) | ((index == run) & (seg == first) & (amount > 0.5))
            bias[:, left : left + LANES] = jnp.where(live, log_count, -jnp.inf)
        tail = count[lands + 2 : lands + 3].astype(i32)
        for left in range(0, half, LANES):
            live = (iota((half, LANES), 0) >= half - tail) & (row[:, left : left + LANES] == first)
            prev_mask[:, left : left + LANES] = jnp.where(live, 0.0, -jnp.inf)
        back_squares[...] = jnp.zeros(back_squares.shape, f32)

    def prepared(head):
        cols = slice(head * HD, (head + 1) * HD)
        index = step * heads + head
        query = dequantized(q_raw, scales, 0, index, cols, scale_rows)
        key = dequantized(k_raw, scales, 1, index, cols, scale_rows)
        value = dequantized(v_raw, scales, 2, index, cols, scale_rows).T
        pieces = []
        for block in range(half // scale_rows):
            at = 2 * HD + 2 + 3 * block
            parts = extras[step, head : head + 1, at : at + 3]
            scale = parts[:, 0:1] + parts[:, 1:2] + parts[:, 2:3]
            raw = prev_raw[block * scale_rows : (block + 1) * scale_rows, cols]
            pieces.append((raw.astype(f32) * scale).astype(bf16))
        prev_key = jnp.concatenate(pieces, axis=0)
        mine = (entry_head == index).astype(f32).astype(bf16)
        land_key = is_early[...] * extras[step, head : head + 1, :HD]
        land_value = is_early[...] * extras[step, head : head + 1, HD : 2 * HD]
        for slot in range(SLOTS):
            pick = picks[slot] * mine
            land_key = land_key + nn_dot(pick, table[:, slot * HD : (slot + 1) * HD])
            land_value = land_value + nn_dot(pick, table[:, (SLOTS + slot) * HD : (SLOTS + slot + 1) * HD])
        land_key = (land_key * inverse[...]).astype(bf16)
        land_value = (land_value * inverse[...]).astype(bf16)
        land_value = jnp.concatenate([land_value, jnp.ones((land_pad, 16), bf16)], axis=1)
        return query, key, value, land_key, land_value, prev_key

    ready = {}

    def scores_of(task):
        head, part = task
        if head not in ready:
            ready[head] = prepared(head)
        query, key, _, land_key, _, prev_key = ready[head]
        rows = slice(part * half, (part + 1) * half)
        mask = far if part else near
        score = nt_dot(key[: (part + 1) * half], query[rows]) * factor + mask[...]
        land_score = nt_dot(land_key, query[rows]) * factor + bias[:, rows]
        if part:
            return score, land_score, None
        return score, land_score, nt_dot(prev_key, query[rows]) * factor + prev_mask[...]

    tasks = [(head, part) for head in range(heads) for part in range(2)]
    scores = [scores_of(task) for task in tasks[:pipeline_depth]]
    for number, (head, part) in enumerate(tasks):
        if number + pipeline_depth < len(tasks):
            scores.append(scores_of(tasks[number + pipeline_depth]))
        cols = slice(head * HD, (head + 1) * HD)
        score, land_score, prev_score = scores[number]
        _, _, value, _, land_value, _ = ready[head]
        top = jnp.maximum(
            jnp.max(score, axis=0, keepdims=True), jnp.max(land_score, axis=0, keepdims=True)
        )
        if part == 0:
            top = jnp.maximum(top, jnp.max(prev_score, axis=0, keepdims=True))
        weight = jnp.exp2(score - top).astype(bf16)
        land_weight = jnp.exp2(land_score - top).astype(bf16)
        found = nn_dot(with_ones(value[:, : (part + 1) * half]), weight)
        found = found + lax.dot_general(
            land_value, land_weight, (((0,), (0,)), ((), ())), preferred_element_type=f32
        )
        total = found[HD : HD + 1]
        if part == 0:
            prev_weight = jnp.exp2(prev_score - top)
            share = 1.0 / (total + jnp.sum(prev_weight, axis=0, keepdims=True))
            open_out[:, cols] = (found[:HD] * share).T
            prev_weights[head] = (prev_weight * share).astype(bf16).T
        else:
            done = found[:HD] * (1.0 / total)
            back_squares[...] += jnp.sum(done * done, axis=0, keepdims=True)
            back_out[:, cols] = done.T * gain[:, cols]


def halo_kernel(opened, prev_weights, gain, back_squares, prev_value, out, squares):
    heads, half = prev_weights.shape[:2]
    found = []
    power = jnp.zeros((half, HD), f32)
    for head in range(heads + pipeline_depth):
        if head < heads:
            found.append(nn_dot(prev_weights[head], prev_value[:, head * HD : (head + 1) * HD]))
        done = head - pipeline_depth
        if done >= 0:
            cols = slice(done * HD, (done + 1) * HD)
            value = opened[:, cols] + found[done]
            power = power + value * value
            out[:, cols] = value * gain[:, cols]
    for start in range(0, half, LANES):
        total = jnp.sum(power[start : start + LANES].T, axis=0, keepdims=True)
        squares[:, start : start + LANES] = total
    squares[:, half:] = back_squares[...]


def scale_kernel(width, count, *refs):
    parts, (front, back, out, ready, sems) = refs[:count], refs[count:]
    total = parts[0][...]
    for ref in parts[1:]:
        total = total + ref[...]
    norm = columns_of(lax.rsqrt(total / width + epsilon))
    half = front.shape[0]
    copies = []
    for part, source in enumerate((front, back)):
        for start in range(0, half, LANES):
            rows = slice(part * half + start, part * half + start + LANES)
            for left in range(0, front.shape[1], LANES):
                cols = slice(left, left + LANES)
                ready[rows, cols] = (source[start : start + LANES, cols] * norm[rows]).astype(bf16)
            copy = pltpu.make_async_copy(ready.at[rows], out.at[rows], sems.at[len(copies)])
            copy.start()
            copies.append(copy)
    for copy in copies:
        copy.wait()


def on_device(q_raw, k_raw, v_raw, block_scales, segment_ids, norm_gain):
    tokens, width = q_raw.shape
    half = tokens // 2
    heads = width // HD
    scale_rows = tokens // block_scales.shape[1]
    devices = lax.axis_size("seq")
    head_devices = lax.axis_size("head")
    entries = devices * heads
    land_pad = -(-(CAP * devices + 3) // 16) * 16
    smem = pl.BlockSpec(memory_space=pltpu.SMEM)
    vmem = pl.BlockSpec(memory_space=pltpu.VMEM)
    hbm = pl.BlockSpec(memory_space=pltpu.HBM)
    sds = jax.ShapeDtypeStruct
    ids = segment_ids.reshape(1, tokens)
    wide = 2 * SLOTS * HD + LANES

    def call(kernel, out_shape, in_specs, args, flops, moved, scratch=(), out_specs=None, limit=vmem_limit, **more):
        return pl.pallas_call(
            kernel,
            out_shape=out_shape,
            in_specs=in_specs,
            out_specs=jax.tree.map(lambda _: vmem, out_shape) if out_specs is None else out_specs,
            scratch_shapes=list(scratch),
            compiler_params=pltpu.CompilerParams(vmem_limit_bytes=limit),
            cost_estimate=pl.CostEstimate(flops=flops, bytes_accessed=moved, transcendentals=0),
            **more,
        )(*args)

    cycle = [(i, (i + 1) % devices) for i in range(devices)]
    prev_key = lax.ppermute(k_raw[half:], "seq", cycle)
    table_pieces = 4
    table, tail_value, extra = call(
        functools.partial(table_kernel, scale_rows, table_pieces),
        [sds((devices, heads, wide), bf16), sds((half, width), bf16), sds((heads, 3 * HD), bf16)],
        [hbm] * 4, (block_scales, ids, k_raw, v_raw),
        64 * tokens * width, 4 * tokens * width, out_specs=[hbm] * 3, limit=whole_vmem,
        scratch=[
            pltpu.SMEM(block_scales.shape, f32), pltpu.VMEM((1, tokens), i32),
            pltpu.VMEM((tokens, width), bf16), pltpu.VMEM((tokens, width), bf16),
            pltpu.VMEM((heads, wide), f32), pltpu.VMEM((devices, heads, wide), bf16), pltpu.VMEM((half, width), bf16),
            pltpu.VMEM((heads, 3 * HD), f32), pltpu.VMEM((heads, 3 * HD), bf16),
            pltpu.SemaphoreType.DMA((table_pieces, 2)), pltpu.SemaphoreType.DMA((2,)), pltpu.SemaphoreType.DMA((table_pieces + 2,)),
        ],
    )
    table = lax.all_to_all(table, "seq", 0, 0, tiled=True)
    table = table.reshape(entries, wide)
    extra = lax.ppermute(extra, "seq", cycle)
    prev_value = lax.ppermute(tail_value, "seq", [(i - 1, i) for i in range(1, devices)])
    place = lax.axis_index("seq").astype(i32).reshape(1)
    gain = norm_gain.reshape(1, width)
    step_heads = 4
    steps = heads // step_heads
    piece = step_heads * HD

    def whole(*shape):
        return pl.BlockSpec(shape, lambda s: (0,) * len(shape))

    rows_in = pl.BlockSpec((tokens, piece), lambda s: (0, s))
    half_rows = pl.BlockSpec((half, piece), lambda s: (0, s))
    opened, prev_weights, back, back_squares = call(
        functools.partial(main_kernel, scale_rows, devices),
        [sds((half, width), f32), sds((heads, half, half), bf16), sds((half, width), f32), sds((1, half), f32)],
        [smem, smem, whole(1, tokens), whole(entries, wide), whole(heads, 3 * HD), pl.BlockSpec((1, piece), lambda s: (0, s))] + [rows_in] * 3 + [half_rows],
        (place, block_scales, ids, table, extra, gain, *(pltpu.with_memory_space_constraint(x, pltpu.HBM) for x in (q_raw, k_raw, v_raw)), prev_key),
        8 * half * tokens * width, 12 * tokens * width, grid=(steps,),
        out_specs=[half_rows, pl.BlockSpec((step_heads, half, half), lambda s: (s, 0, 0)), half_rows, whole(1, half)],
        scratch=[
            pltpu.VMEM((half, half), f32), pltpu.VMEM((tokens, half), f32),
            pltpu.VMEM((SLOTS, land_pad, entries), bf16), pltpu.VMEM((land_pad, tokens), f32),
            pltpu.VMEM((land_pad, HD), f32), pltpu.VMEM((half, half), f32), pltpu.VMEM((steps, step_heads, 3 * HD), f32), pltpu.VMEM((land_pad, HD), f32),
        ],
    )
    front, squares = call(
        halo_kernel, [sds((half, width), f32), sds((1, tokens), f32)],
        [vmem] * 5, (opened, prev_weights, gain, back_squares, prev_value),
        half * half * width * 2, 8 * tokens * width,
    )
    pairs = head_devices & (head_devices - 1) == 0
    parts = [squares] + [
        lax.ppermute(squares, "head", [(i, i ^ d if pairs else (i + d) % head_devices) for i in range(head_devices)])
        for d in range(1, head_devices)
    ]
    return call(
        functools.partial(scale_kernel, width * head_devices, head_devices), sds((tokens, width), bf16),
        [vmem] * (head_devices + 2), (*parts, front, back),
        3 * tokens * width, 6 * tokens * width, out_specs=pl.BlockSpec(memory_space=pl.ANY),
        scratch=[pltpu.VMEM((tokens, width), bf16), pltpu.SemaphoreType.DMA((tokens // LANES,))],
    )


def solution(mesh):
    in_specs = (
        P("seq", "head"), P("seq", "head"), P("seq", "head"),
        P(None, "seq", "head"), P("seq"), P("head"),
    )

    return jax.shard_map(on_device, mesh=mesh, in_specs=in_specs, out_specs=P("seq", "head"), check_vma=False)
```

```python
import functools
import math

import jax
import jax.numpy as jnp
from jax import lax
from jax.experimental import pallas as pl
from jax.experimental.pallas import tpu as pltpu
from jax.sharding import PartitionSpec as P


HD = 128
CAP = 4
LANES = 128
SLOTS = CAP + 1
EARLY = CAP + 1
epsilon = 1e-06
factor = math.log2(math.e) / math.sqrt(HD)
f32 = jnp.float32
bf16 = jnp.bfloat16
i32 = jnp.int32
vmem_limit = 20 * 2**20
whole_vmem = 60 * 1024 * 2**10
pipeline_depth = 2


def nt_dot(a, b):
    return lax.dot_general(a, b, (((1,), (1,)), ((), ())), preferred_element_type=f32)


def nn_dot(a, b):
    return jnp.dot(a, b, preferred_element_type=f32)


def iota(shape, axis):
    return lax.broadcasted_iota(i32, shape, axis)


def columns_of(row):
    pieces = []
    for start in range(0, row.shape[1], LANES):
        pieces.append(jnp.broadcast_to(row[:, start : start + LANES], (LANES, LANES)).T)
    return jnp.concatenate(pieces, axis=0)


def dequantized(raw, scales, which, head, cols, scale_rows, first=0):
    parts = []
    for piece in range(raw.shape[0] // scale_rows):
        rows = slice(piece * scale_rows, (piece + 1) * scale_rows)
        parts.append((raw[rows, cols].astype(f32) * scales[which, first + piece, head]).astype(bf16))
    return jnp.concatenate(parts, axis=0)


def table_kernel(
    scale_rows, pieces, scales_in, ids_in, k_raw, v_raw, table, tail_value, relay_value, extra_out,
    scales, ids, keys, values, sums, packed, tails, extra, extra_packed, sems, small_sems, out_sems,
):
    tokens = ids.shape[1]
    half = tokens // 2
    heads = sums.shape[0]
    piece = heads * HD // pieces
    small = [
        pltpu.make_async_copy(scales_in, scales, small_sems.at[0]),
        pltpu.make_async_copy(ids_in, ids, small_sems.at[1]),
    ]
    for copy in small:
        copy.start()
    copies = []
    for number in range(pieces):
        cols = slice(number * piece, (number + 1) * piece)
        for which, (source, target) in enumerate(((k_raw, keys), (v_raw, values))):
            copy = pltpu.make_async_copy(source.at[:, cols], target.at[:, cols], sems.at[number, which])
            copy.start()
            copies.append(copy)
    for copy in small:
        copy.wait()
    row = ids[...]
    local = row - row[:, 0:1]
    last = local[:, tokens - 1 :]
    slot = iota((2 * 8, tokens), 0)
    token = iota((2 * 8, tokens), 1)
    picked = (slot <= CAP) & (local == slot)
    picked = picked | ((slot == EARLY) & (local == last) & (token < half))
    picked = picked.astype(f32)
    pick = picked.astype(bf16)
    count = jnp.sum(picked, axis=1, keepdims=True).astype(i32)
    lane = iota((heads, LANES), 1)
    head_row = iota((heads, LANES), 0)
    meta = jnp.zeros((heads, LANES), i32)
    for index in range(SLOTS):
        seg = row[:, 0:1] + index
        number = count[index : index + 1]
        for place, value in enumerate((seg & 127, seg >> 7, number & 127, number >> 7)):
            meta = jnp.where(lane == 4 * index + place, value, meta)
    sums[:, 2 * SLOTS * HD :] = meta.astype(f32)
    number = count[EARLY : EARLY + 1]
    meta = jnp.where(lane == 0, number & 127, jnp.where(lane == 1, number >> 7, 0))
    tail_blocks = half // scale_rows
    scale = jnp.zeros((heads, LANES), f32)
    part = jnp.zeros((heads, LANES), i32)
    for block in range(tail_blocks):
        for head in range(heads):
            value = scales[1, scales.shape[1] - tail_blocks + block, head]
            here = (lane >= 2 + 3 * block) & (lane < 5 + 3 * block)
            scale = jnp.where(here & (head_row == head), value, scale)
        for place in range(3):
            part = jnp.where(lane == 2 + 3 * block + place, place, part)
    high = scale.astype(bf16).astype(f32)
    middle = (scale - high).astype(bf16).astype(f32)
    low = scale - high - middle
    scale = jnp.where(part == 0, high, jnp.where(part == 1, middle, low))
    extra[:, 2 * HD :] = jnp.where(lane < 2, meta.astype(f32), scale)
    writes = []
    for number in range(pieces):
        found = []
        for which, source in enumerate((keys, values)):
            copies[2 * number + which].wait()
            for head in range(number * piece // HD, (number + 1) * piece // HD):
                cols = slice(head * HD, (head + 1) * HD)
                value = dequantized(source, scales, 1 + which, head, cols, scale_rows)
                if which:
                    tails[:, cols] = value[half:]
                found.append((head, which, nn_dot(pick, value)))
        for head, which, total in found:
            for index in range(SLOTS):
                where = slice((which * SLOTS + index) * HD, (which * SLOTS + index + 1) * HD)
                sums[head : head + 1, where] = total[index : index + 1]
            extra[head : head + 1, which * HD : (which + 1) * HD] = total[EARLY : EARLY + 1]
        cols = slice(number * piece, (number + 1) * piece)
        target = tail_value.at[:, cols] if number < pieces - 1 else relay_value
        copy = pltpu.make_async_copy(tails.at[:, cols], target, out_sems.at[number])
        copy.start()
        writes.append(copy)
    packed[...] = jnp.broadcast_to(sums[...].astype(bf16)[None], packed.shape)
    extra_packed[...] = extra[...].astype(bf16)
    for number, (source, target) in enumerate(((packed, table), (extra_packed, extra_out))):
        copy = pltpu.make_async_copy(source, target, out_sems.at[pieces + number])
        copy.start()
        writes.append(copy)
    for copy in writes:
        copy.wait()


def with_ones(value):
    return jnp.concatenate([value, jnp.ones((16, value.shape[1]), bf16)], axis=0)


def main_kernel(
    scale_rows, device_count,
    place, scales, ids, table, extra, gain, q_raw, k_raw, v_raw, prev_raw,
    open_out, prev_weights, back_out, back_squares,
    near, far, picks, bias, inverse, prev_mask, extras, is_early,
):
    step = pl.program_id(0)
    tokens = ids.shape[1]
    half = tokens // 2
    heads = q_raw.shape[1] // HD
    lands = CAP * device_count
    land_pad, entries = picks.shape[1:]
    all_heads = entries // device_count
    entry = iota((1, entries), 1)
    entry_device = entry // all_heads
    entry_head = entry - entry_device * all_heads

    @pl.when(step == 0)
    def _():
        me = place[0]
        row = ids[...]
        first = row[:, 0:1]
        column = columns_of(row)
        for mask, start, width in ((near, 0, half), (far, half, tokens)):
            for left in range(0, half, LANES):
                query = iota((width, LANES), 1) + (start + left)
                live = column[:width] == row[:, start + left : start + left + LANES]
                live = live & (iota((width, LANES), 0) <= query)
                mask[:, left : left + LANES] = jnp.where(live, 0.0, -jnp.inf)
        info = table[:, 2 * SLOTS * HD :].astype(f32).T
        land = iota((land_pad, entries), 0)
        count = jnp.zeros((land_pad, 1), f32)
        for index in range(SLOTS):
            seg = info[4 * index : 4 * index + 1] + 128.0 * info[4 * index + 1 : 4 * index + 2]
            number = info[4 * index + 2 : 4 * index + 3] + 128.0 * info[4 * index + 3 : 4 * index + 4]
            is_open = seg == first.astype(f32)
            picked = (land < lands) & (land.astype(f32) == seg)
            picked = picked | ((land == lands) & is_open & (entry_device < me - 1))
            picked = picked | ((land == lands + 1) & is_open & (entry_device < me))
            picked = picked | ((land == lands + 2) & is_open & (entry_device == me - 1))
            picked = picked.astype(f32)
            picks[index] = picked.astype(bf16)
            count = count + jnp.sum(
                picked * jnp.where(entry_head == 0, number, 0.0), axis=1, keepdims=True
            )
        early = ((iota((land_pad, HD), 0) == lands) & (me > 0)).astype(f32)
        is_early[...] = early
        info = extra[...].astype(f32)
        for group in range(all_heads // heads):
            extras[group] = info[group * heads : (group + 1) * heads]
        count = count + early[:, 0:1] * (info[0:1, 2 * HD : 2 * HD + 1] + 128.0 * info[0:1, 2 * HD + 1 : 2 * HD + 2])
        inverse[...] = jnp.broadcast_to(1.0 / jnp.maximum(count, 1.0), inverse.shape)
        amount = jnp.broadcast_to(count, (land_pad, LANES))
        log_count = jnp.log2(jnp.maximum(amount, 1.0))
        for left in range(0, tokens, LANES):
            seg = row[:, left : left + LANES]
            index = iota((land_pad, LANES), 0)
            run = lands if left < half else lands + 1
            live = ((index < lands) & (index < seg)) | ((index == run) & (seg == first) & (amount > 0.5))
            bias[:, left : left + LANES] = jnp.where(live, log_count, -jnp.inf)
        tail = count[lands + 2 : lands + 3].astype(i32)
        for left in range(0, half, LANES):
            live = (iota((half, LANES), 0) >= half - tail) & (row[:, left : left + LANES] == first)
            prev_mask[:, left : left + LANES] = jnp.where(live, 0.0, -jnp.inf)
        back_squares[...] = jnp.zeros(back_squares.shape, f32)

    def prepared(head):
        cols = slice(head * HD, (head + 1) * HD)
        index = step * heads + head
        query = dequantized(q_raw, scales, 0, index, cols, scale_rows)
        key = dequantized(k_raw, scales, 1, index, cols, scale_rows)
        value = dequantized(v_raw, scales, 2, index, cols, scale_rows).T
        pieces = []
        for block in range(half // scale_rows):
            at = 2 * HD + 2 + 3 * block
            parts = extras[step, head : head + 1, at : at + 3]
            scale = parts[:, 0:1] + parts[:, 1:2] + parts[:, 2:3]
            raw = prev_raw[block * scale_rows : (block + 1) * scale_rows, cols]
            pieces.append((raw.astype(f32) * scale).astype(bf16))
        prev_key = jnp.concatenate(pieces, axis=0)
        mine = (entry_head == index).astype(f32).astype(bf16)
        land_key = is_early[...] * extras[step, head : head + 1, :HD]
        land_value = is_early[...] * extras[step, head : head + 1, HD : 2 * HD]
        for slot in range(SLOTS):
            pick = picks[slot] * mine
            land_key = land_key + nn_dot(pick, table[:, slot * HD : (slot + 1) * HD])
            land_value = land_value + nn_dot(pick, table[:, (SLOTS + slot) * HD : (SLOTS + slot + 1) * HD])
        land_key = (land_key * inverse[...]).astype(bf16)
        land_value = (land_value * inverse[...]).astype(bf16)
        land_value = jnp.concatenate([land_value, jnp.ones((land_pad, 16), bf16)], axis=1)
        return query, key, value, land_key, land_value, prev_key

    ready = {}

    def scores_of(task):
        head, part = task
        if head not in ready:
            ready[head] = prepared(head)
        query, key, _, land_key, _, prev_key = ready[head]
        rows = slice(part * half, (part + 1) * half)
        mask = far if part else near
        score = nt_dot(key[: (part + 1) * half], query[rows]) * factor + mask[...]
        land_score = nt_dot(land_key, query[rows]) * factor + bias[:, rows]
        if part:
            return score, land_score, None
        return score, land_score, nt_dot(prev_key, query[rows]) * factor + prev_mask[...]

    tasks = [(head, part) for head in range(heads) for part in range(2)]
    scores = [scores_of(task) for task in tasks[:pipeline_depth]]
    for number, (head, part) in enumerate(tasks):
        if number + pipeline_depth < len(tasks):
            scores.append(scores_of(tasks[number + pipeline_depth]))
        cols = slice(head * HD, (head + 1) * HD)
        score, land_score, prev_score = scores[number]
        _, _, value, _, land_value, _ = ready[head]
        top = jnp.maximum(
            jnp.max(score, axis=0, keepdims=True), jnp.max(land_score, axis=0, keepdims=True)
        )
        if part == 0:
            top = jnp.maximum(top, jnp.max(prev_score, axis=0, keepdims=True))
        weight = jnp.exp2(score - top).astype(bf16)
        land_weight = jnp.exp2(land_score - top).astype(bf16)
        found = nn_dot(with_ones(value[:, : (part + 1) * half]), weight)
        found = found + lax.dot_general(
            land_value, land_weight, (((0,), (0,)), ((), ())), preferred_element_type=f32
        )
        total = found[HD : HD + 1]
        if part == 0:
            prev_weight = jnp.exp2(prev_score - top)
            share = 1.0 / (total + jnp.sum(prev_weight, axis=0, keepdims=True))
            open_out[:, cols] = (found[:HD] * share).T
            prev_weights[head] = (prev_weight * share).astype(bf16).T
        else:
            done = found[:HD] * (1.0 / total)
            back_squares[...] += jnp.sum(done * done, axis=0, keepdims=True)
            back_out[:, cols] = done.T * gain[:, cols]


def halo_kernel(first, opened, prev_weights, gain, prev_value, *refs):
    half = opened.shape[0]
    if first:
        before, back_squares, out, squares = refs
        power = before[...]
    else:
        out, so_far = refs
        power = jnp.zeros((half, HD), f32)
    found = []
    count = prev_value.shape[1] // HD
    for index in range(count + pipeline_depth):
        if index < count:
            found.append(nn_dot(prev_weights[first + index], prev_value[:, index * HD : (index + 1) * HD]))
        done = index - pipeline_depth
        if done >= 0:
            cols = slice((first + done) * HD, (first + done + 1) * HD)
            value = opened[:, cols] + found[done]
            power = power + value * value
            out[:, done * HD : (done + 1) * HD] = value * gain[:, cols]
    if first:
        for start in range(0, half, LANES):
            total = jnp.sum(power[start : start + LANES].T, axis=0, keepdims=True)
            squares[:, start : start + LANES] = total
        squares[:, half:] = back_squares[...]
    else:
        so_far[...] = power


def scale_kernel(width, count, *refs):
    parts, (front, rest, back, out, ready, sems) = refs[:count], refs[count:]
    total = parts[0][...]
    for ref in parts[1:]:
        total = total + ref[...]
    norm = columns_of(lax.rsqrt(total / width + epsilon))
    half = front.shape[0]
    copies = []
    for part, source in enumerate((front, back)):
        for start in range(0, half, LANES):
            rows = slice(part * half + start, part * half + start + LANES)
            for left in range(0, back.shape[1], LANES):
                cols = slice(left, left + LANES)
                block, at = (rest, left - front.shape[1]) if part == 0 and left >= front.shape[1] else (source, left)
                value = block[start : start + LANES, at : at + LANES] * norm[rows]
                ready[rows, cols] = value.astype(bf16)
            copy = pltpu.make_async_copy(ready.at[rows], out.at[rows], sems.at[len(copies)])
            copy.start()
            copies.append(copy)
    for copy in copies:
        copy.wait()


def on_device(q_raw, k_raw, v_raw, block_scales, segment_ids, norm_gain):
    tokens, width = q_raw.shape
    half = tokens // 2
    heads = width // HD
    scale_rows = tokens // block_scales.shape[1]
    devices = lax.axis_size("seq")
    head_devices = lax.axis_size("head")
    entries = devices * heads
    land_pad = -(-(CAP * devices + 3) // 16) * 16
    smem = pl.BlockSpec(memory_space=pltpu.SMEM)
    vmem = pl.BlockSpec(memory_space=pltpu.VMEM)
    hbm = pl.BlockSpec(memory_space=pltpu.HBM)
    sds = jax.ShapeDtypeStruct
    ids = segment_ids.reshape(1, tokens)
    wide = 2 * SLOTS * HD + LANES

    def call(kernel, out_shape, in_specs, args, flops, moved, scratch=(), out_specs=None, limit=vmem_limit, **more):
        return pl.pallas_call(
            kernel,
            out_shape=out_shape,
            in_specs=in_specs,
            out_specs=jax.tree.map(lambda _: vmem, out_shape) if out_specs is None else out_specs,
            scratch_shapes=list(scratch),
            compiler_params=pltpu.CompilerParams(vmem_limit_bytes=limit),
            cost_estimate=pl.CostEstimate(flops=flops, bytes_accessed=moved, transcendentals=0),
            **more,
        )(*args)

    cycle = [(i, (i + 1) % devices) for i in range(devices)]
    prev_key = lax.ppermute(k_raw[half:], "seq", cycle)
    table_pieces = 2
    relay_width = width // table_pieces
    straight = width - relay_width
    table, tail_value, relay_value, extra = call(
        functools.partial(table_kernel, scale_rows, table_pieces),
        [sds((devices, heads, wide), bf16), sds((half, straight), bf16), sds((half, relay_width), bf16), sds((heads, 3 * HD), bf16)],
        [hbm] * 4, (block_scales, ids, k_raw, v_raw),
        64 * tokens * width, 4 * tokens * width, out_specs=[hbm] * 4, limit=whole_vmem,
        scratch=[
            pltpu.SMEM(block_scales.shape, f32), pltpu.VMEM((1, tokens), i32),
            pltpu.VMEM((tokens, width), bf16), pltpu.VMEM((tokens, width), bf16),
            pltpu.VMEM((heads, wide), f32), pltpu.VMEM((devices, heads, wide), bf16), pltpu.VMEM((half, width), bf16),
            pltpu.VMEM((heads, 3 * HD), f32), pltpu.VMEM((heads, 3 * HD), bf16),
            pltpu.SemaphoreType.DMA((table_pieces, 2)), pltpu.SemaphoreType.DMA((2,)), pltpu.SemaphoreType.DMA((table_pieces + 2,)),
        ],
    )
    table = lax.all_to_all(table, "seq", 0, 0, tiled=True)
    table = table.reshape(entries, wide)
    prev_value = lax.ppermute(tail_value, "seq", [(i - 1, i) for i in range(1, devices)])
    prev_rest = lax.ppermute(relay_value, "seq", [(i - 1, i) for i in range(1, devices)])
    extra = lax.ppermute(extra, "seq", cycle)
    place = lax.axis_index("seq").astype(i32).reshape(1)
    gain = norm_gain.reshape(1, width)
    step_heads = 4
    steps = heads // step_heads
    piece = step_heads * HD

    def whole(*shape):
        return pl.BlockSpec(shape, lambda s: (0,) * len(shape))

    rows_in = pl.BlockSpec((tokens, piece), lambda s: (0, s))
    half_rows = pl.BlockSpec((half, piece), lambda s: (0, s))
    opened, prev_weights, back, back_squares = call(
        functools.partial(main_kernel, scale_rows, devices),
        [sds((half, width), f32), sds((heads, half, half), bf16), sds((half, width), f32), sds((1, half), f32)],
        [smem, smem, whole(1, tokens), whole(entries, wide), whole(heads, 3 * HD), pl.BlockSpec((1, piece), lambda s: (0, s))] + [rows_in] * 3 + [half_rows],
        (place, block_scales, ids, table, extra, gain, *(pltpu.with_memory_space_constraint(x, pltpu.HBM) for x in (q_raw, k_raw, v_raw)), prev_key),
        8 * half * tokens * width, 12 * tokens * width, grid=(steps,),
        out_specs=[half_rows, pl.BlockSpec((step_heads, half, half), lambda s: (s, 0, 0)), half_rows, whole(1, half)],
        scratch=[
            pltpu.VMEM((half, half), f32), pltpu.VMEM((tokens, half), f32),
            pltpu.VMEM((SLOTS, land_pad, entries), bf16), pltpu.VMEM((land_pad, tokens), f32),
            pltpu.VMEM((land_pad, HD), f32), pltpu.VMEM((half, half), f32), pltpu.VMEM((steps, step_heads, 3 * HD), f32), pltpu.VMEM((land_pad, HD), f32),
        ],
    )
    front, power = call(
        functools.partial(halo_kernel, 0), [sds((half, straight), f32), sds((half, HD), f32)],
        [vmem] * 4, (opened, prev_weights, gain, prev_value),
        half * half * straight * 2, 8 * tokens * width,
    )
    rest, squares = call(
        functools.partial(halo_kernel, straight // HD), [sds((half, relay_width), f32), sds((1, tokens), f32)],
        [vmem] * 6, (opened, prev_weights, gain, prev_rest, power, back_squares),
        half * half * relay_width * 2, 2 * tokens * width,
    )
    pairs = head_devices & (head_devices - 1) == 0
    parts = [squares] + [
        lax.ppermute(squares, "head", [(i, i ^ d if pairs else (i + d) % head_devices) for i in range(head_devices)])
        for d in range(1, head_devices)
    ]
    return call(
        functools.partial(scale_kernel, width * head_devices, head_devices), sds((tokens, width), bf16),
        [vmem] * (head_devices + 3), (*parts, front, rest, back),
        3 * tokens * width, 6 * tokens * width, out_specs=pl.BlockSpec(memory_space=pl.ANY),
        scratch=[pltpu.VMEM((tokens, width), bf16), pltpu.SemaphoreType.DMA((tokens // LANES,))],
    )


def solution(mesh):
    in_specs = (
        P("seq", "head"), P("seq", "head"), P("seq", "head"),
        P(None, "seq", "head"), P("seq"), P("head"),
    )

    return jax.shard_map(on_device, mesh=mesh, in_specs=in_specs, out_specs=P("seq", "head"), check_vma=False)
```
